256 devices in a mesh: inner: 8 (over y, core), outer: 32 (over z, x).
Axes of the slice: x: 4, y: 4, z: 8, core: 2. Of those that a mesh axis runs over, the one named last changes fastest.
Arguments:
- query_rows: bfloat16 [131072, 512], P(('outer', 'inner')), may hold values from -6 to 6
- key_rows: bfloat16 [131072, 512], P(('outer', 'inner')), may hold values from -6 to 6
- value_rows: bfloat16 [131072, 512], P(('outer', 'inner')), may hold values from -6 to 6
- level_ids: int32 [131072], P(('outer', 'inner')), may hold values from 0 to 15
- level_table: float32 [16, 16, 4], replicated, may hold values from 0.1 to 1
Outputs:
- attended: bfloat16 [131072, 512], P(('outer', 'inner'))
The draws below stay inside these ranges and needn't reach their ends.
All inputs are finite; a program needn't handle non-finite values.
Results may differ from the reference program's by a relative error of at most 0.0049.
Values sent between devices are 32-bit elements; how exact they have to be, the bound alone decides.
A program may use at most 64 MiB of HBM per device.

```python
import math
import jax
import jax.numpy as jnp
from jax import lax

HEADS = 4
HD = 128
SPAN = 128
LEVELS = 16
CLASSES = 16
TOK_DEV = 512
TOKENS = 131072
N_INNER = 8
N_OUTER = 32


def plant(entries, key, low, top_value):
    longest = entries.shape.index(max(entries.shape))
    spots = []
    for shift in (0, 1):
        where = [jax.random.randint(jax.random.fold_in(key, axis), (), 0, length) for axis, length in enumerate(entries.shape)]
        where[longest] = (where[longest] + shift) % entries.shape[longest]
        spots.append(tuple(where))
    return entries.at[spots[0]].set(low).at[spots[1]].set(top_value)


def block_scale(own_key, extent, split, smallest, top_value):
    def one(axis_at, blocks):
        steps = jax.random.uniform(jax.random.fold_in(jax.random.fold_in(own_key, 6), axis_at), (blocks,), jnp.float32, smallest / len(split), top_value / len(split))
        return jnp.repeat(jnp.exp(steps), extent[axis_at] // blocks).reshape((-1,) + (1,) * (len(extent) - axis_at - 1))

    gain = one(*split[0])
    for cut in split[1:]:
        gain = gain * one(*cut)
    return gain


def gaussian(key, dims, spread, limit, cuts=(), kind=jnp.bfloat16):
    array = jax.random.normal(key, dims, jnp.float32) * spread
    if len(cuts) > 0:
        array = block_scale(key, dims, cuts, -0.22, 0.18) * array
    return jnp.clip(array, min=-limit, max=limit).astype(kind)


def setup_inputs(seed: int = 0) -> dict:
    arg_keys = jax.random.split(jax.random.key(seed), 6)
    return {
        "query_rows": gaussian(arg_keys[0], (TOKENS, HEADS * HD), 1.0, 6.0, ((0, 256),)),
        "key_rows": gaussian(arg_keys[1], (TOKENS, HEADS * HD), 1.0, 6.0, ((0, 256),)),
        "value_rows": gaussian(arg_keys[2], (TOKENS, HEADS * HD), 1.0, 6.0, ((0, 256),)),
        "level_ids": plant(jax.random.randint(arg_keys[3], (TOKENS,), 0, CLASSES), jax.random.fold_in(arg_keys[3], 1), 0, CLASSES - 1).astype(jnp.int32),
        "level_table": jnp.clip(jnp.exp(jax.random.uniform(arg_keys[4], (CLASSES, LEVELS, HEADS), jnp.float32, math.log(0.1), math.log(1.0))), 0.1, 1.0),
    }


norm_eps = 1e-06
precise = lax.Precision.HIGHEST

def left_selectors(count, own_rows, level_bits):
    columns = jnp.arange(count, dtype=jnp.int32)
    result = []
    for bit_pos in range(level_bits):
        lower = own_rows >> bit_pos + 1 << bit_pos + 1
        upper = own_rows >> bit_pos << bit_pos
        active = own_rows >> bit_pos & 1 == 1
        inside = (columns[None, :] >= lower[:, None]) & (columns[None, :] < upper[:, None]) & active[:, None]
        result.append(inside.astype(jnp.float32))
    return result

def local_output(query_rows, key_rows, value_rows, weights_tok, cross_states):
    token_count = query_rows.shape[0]
    span_count = token_count // SPAN
    level_bits = span_count.bit_length() - 1
    shape_four = (span_count, SPAN, HEADS, HD)
    query_blocks = query_rows.reshape(shape_four).astype(jnp.float32)
    key_blocks = key_rows.reshape(shape_four).astype(jnp.float32)
    value_blocks = value_rows.reshape(shape_four).astype(jnp.float32)
    level_blocks = weights_tok.reshape(span_count, SPAN, LEVELS, HEADS)
    span_states = jnp.einsum('cthd,cthe->chde', key_blocks, value_blocks)
    scores = jnp.einsum('cthd,cshd->chts', query_blocks, key_blocks)
    position = jnp.arange(SPAN, dtype=jnp.int32)
    causal = position[:, None] >= position[None, :]
    scale_now = jnp.transpose(level_blocks[:, :, 0, :], (0, 2, 1))[..., None]
    weighted = lax.optimization_barrier(jnp.where(causal, scores * scale_now, 0.0).astype(jnp.bfloat16))
    unnormed = jnp.einsum('chts,cshd->cthd', weighted.astype(jnp.float32), value_blocks)
    flat = span_states.reshape(span_count, -1)
    selectors = left_selectors(span_count, jnp.arange(span_count, dtype=jnp.int32), level_bits)
    for bit_pos in range(level_bits):
        left_block = jnp.dot(selectors[bit_pos], flat, precision=precise).reshape(span_states.shape)
        left_block = lax.optimization_barrier(left_block.astype(jnp.bfloat16)).astype(jnp.float32)
        partial_out = jnp.einsum('cthd,chde->cthe', query_blocks, left_block)
        unnormed = unnormed + level_blocks[:, :, 1 + bit_pos, :, None] * partial_out
    unnormed = unnormed.reshape(token_count, HEADS, HD)
    query_heads = query_rows.reshape(token_count, HEADS, HD).astype(jnp.float32)
    for bit_pos in range(len(cross_states)):
        partial_out = jnp.einsum('thd,hde->the', query_heads, cross_states[bit_pos].astype(jnp.float32))
        unnormed = unnormed + weights_tok[:, 1 + level_bits + bit_pos, :, None] * partial_out
    mean_square = lax.optimization_barrier(jnp.mean(unnormed * unnormed, axis=-1, keepdims=True))
    normed = unnormed * lax.rsqrt(mean_square + norm_eps)
    return normed.reshape(token_count, HEADS * HD).astype(jnp.bfloat16)

def reference(query_rows, key_rows, value_rows, level_ids, level_table):
    shards = N_INNER * N_OUTER
    cross_bits = shards.bit_length() - 1
    shard_ids = jnp.arange(shards, dtype=jnp.int32)

    def shard_state(shard):
        start = (shard * TOK_DEV).astype(jnp.int32)
        keys_here = lax.dynamic_slice_in_dim(key_rows, start, TOK_DEV, 0).reshape(TOK_DEV, HEADS, HD)
        values_here = lax.dynamic_slice_in_dim(value_rows, start, TOK_DEV, 0).reshape(TOK_DEV, HEADS, HD)
        return jnp.einsum('thd,the->hde', keys_here.astype(jnp.float32), values_here.astype(jnp.float32))
    states = lax.map(shard_state, shard_ids)
    prefix = jnp.concatenate([jnp.zeros((1, HEADS, HD, HD), jnp.float32), jnp.cumsum(states, axis=0)], axis=0)

    def shard_out(shard):
        start = (shard * TOK_DEV).astype(jnp.int32)
        queries_here = lax.dynamic_slice_in_dim(query_rows, start, TOK_DEV, 0)
        keys_here = lax.dynamic_slice_in_dim(key_rows, start, TOK_DEV, 0)
        values_here = lax.dynamic_slice_in_dim(value_rows, start, TOK_DEV, 0)
        ids_here = lax.dynamic_slice_in_dim(level_ids, start, TOK_DEV, 0)
        weights_tok = level_table[ids_here]
        cross_states = []
        for bit_pos in range(cross_bits):
            upper = shard >> bit_pos << bit_pos
            lower = shard >> bit_pos + 1 << bit_pos + 1
            active = (shard >> bit_pos & 1).astype(jnp.float32)
            cross_states.append(((prefix[upper] - prefix[lower]) * active).astype(jnp.bfloat16))
        return local_output(queries_here, keys_here, values_here, weights_tok, cross_states)
    blocks = lax.map(shard_out, shard_ids)
    return blocks.reshape(TOKENS, HEADS * HD)
```

```python
import jax
import jax.numpy as jnp
from jax import lax
from jax.experimental import pallas as pl
from jax.experimental.pallas import tpu as pltpu
from jax.sharding import PartitionSpec as P

HEADS = 4
HD = 128
SPAN = 128
LEVELS = 16
CLASSES = 16
TOK = 512
SPANS = TOK // SPAN
ROWS = HEADS * HD
PLANE = 32
PLANE_BITS = 5
LAYERS = 8
LAYER_BITS = 3
CH = ROWS // PLANE
EPS = 1e-06
MESH = pl.DeviceIdType.MESH
F32 = jnp.float32
BF16 = jnp.bfloat16


def chunk_row(m):
    return pl.multiple_of(((m % 2) * (PLANE // 2) + m // 2) * CH, CH)


def kernel(
    q_hbm, k_hbm, v_hbm, ids_ref, table_ref, o_ref,
    q, k, v, state, parts, tree, zparts, ztree, left, lam, acc, scaled,
    in_sem, rs_send, rs_recv, lv_send, lv_recv, z_send, z_recv,
):
    outer = lax.axis_index("outer")
    inner = lax.axis_index("inner")
    z = outer // 4
    m = (outer % 4) * 8 + inner

    def plane_dev(mm):
        return {"outer": z * 4 + mm // 8, "inner": mm % 8}

    def layer_dev(zz):
        return {"outer": zz * 4 + outer % 4, "inner": inner}

    loads = [
        pltpu.make_async_copy(src, dst, in_sem.at[n])
        for n, (src, dst) in enumerate(((k_hbm, k), (v_hbm, v), (q_hbm, q)))
    ]
    for c in loads:
        c.start()

    barrier = pltpu.get_barrier_semaphore()

    def greet_plane(j, _):
        pl.semaphore_signal(barrier, inc=1, device_id=plane_dev((m + j) % PLANE), device_id_type=MESH)
        return 0

    def greet_layer(j, _):
        pl.semaphore_signal(barrier, inc=1, device_id=layer_dev((z + j) % LAYERS), device_id_type=MESH)
        return 0

    lax.fori_loop(1, PLANE, greet_plane, 0)
    lax.fori_loop(1, LAYERS, greet_layer, 0)

    def head(h):
        return slice(h * HD, (h + 1) * HD)

    def contract_tokens(a, b):
        return lax.dot_general(a, b, (((0,), (0,)), ((), ())), preferred_element_type=F32)

    loads[0].wait()
    loads[1].wait()
    for h in range(HEADS):
        state[head(h), :] = contract_tokens(k[:, head(h)], v[:, head(h)])

    pl.semaphore_wait(barrier, PLANE - 1 + LAYERS - 1)

    my_row = chunk_row(m)

    def send_chunk(j, _):
        mm = (m + j) % PLANE
        pltpu.make_async_remote_copy(
            src_ref=state.at[pl.ds(chunk_row(mm), CH)],
            dst_ref=parts.at[pl.ds(pl.multiple_of(m * CH, CH), CH)],
            send_sem=rs_send, recv_sem=rs_recv,
            device_id=plane_dev(mm), device_id_type=MESH,
        ).start()
        return 0

    lax.fori_loop(1, PLANE, send_chunk, 0)
    parts[pl.ds(pl.multiple_of(m * CH, CH), CH), :] = state[pl.ds(my_row, CH), :]

    loads[2].wait()
    classes = lax.broadcasted_iota(jnp.int32, (CLASSES, SPAN), 0)
    causal = lax.broadcasted_iota(jnp.int32, (SPAN, SPAN), 0) >= lax.broadcasted_iota(
        jnp.int32, (SPAN, SPAN), 1
    )
    span_rows = [slice(c * SPAN, (c + 1) * SPAN) for c in range(SPANS)]
    for c in range(SPANS):
        hot = (ids_ref[c : c + 1, :] == classes).astype(F32)
        lam[span_rows[c], :] = lax.dot_general(
            hot, table_ref[...], (((0,), (0,)), ((), ())),
            precision=lax.Precision.HIGHEST, preferred_element_type=F32,
        )

    def weight(rows, level, h):
        n = level * HEADS + h
        return lam[rows, n : n + 1]

    for h in range(HEADS):
        spans = [contract_tokens(k[span_rows[c], head(h)], v[span_rows[c], head(h)]) for c in range(3)]
        first = [None, spans[0].astype(BF16), None, spans[2].astype(BF16)]
        second = (spans[0] + spans[1]).astype(BF16)
        for c in range(SPANS):
            rows = span_rows[c]
            q_now = q[rows, head(h)]
            scores = lax.dot_general(
                q_now, k[rows, head(h)], (((1,), (1,)), ((), ())), preferred_element_type=F32
            )
            weighted = jnp.where(causal, scores * weight(rows, 0, h), 0.0).astype(BF16)
            out = jnp.dot(weighted, v[rows, head(h)], preferred_element_type=F32)
            if c % 2 == 1:
                out += weight(rows, 1, h) * jnp.dot(q_now, first[c], preferred_element_type=F32)
            if c >= 2:
                out += weight(rows, 2, h) * jnp.dot(q_now, second, preferred_element_type=F32)
            acc[rows, head(h)] = out

    def plane_wait(send):
        c = pltpu.make_async_remote_copy(
            src_ref=state.at[pl.ds(0, (PLANE - 1) * CH)],
            dst_ref=parts.at[pl.ds(0, (PLANE - 1) * CH)],
            send_sem=rs_send, recv_sem=rs_recv,
            device_id=plane_dev((m + 1) % PLANE), device_id_type=MESH,
        )
        c.wait_send() if send else c.wait_recv()

    plane_wait(False)
    base = [0, 0, 16, 24, 28, 30]
    level = [parts[n * CH : (n + 1) * CH, :] for n in range(PLANE)]
    for b in range(1, PLANE_BITS + 1):
        level = [level[2 * n] + level[2 * n + 1] for n in range(len(level) // 2)]
        for n, value in enumerate(level):
            at = (base[b] + n) * CH
            tree[at : at + CH, :] = value

    total = tree.at[pl.ds(base[PLANE_BITS] * CH, CH)]

    def z_copy(step):
        return pltpu.make_async_remote_copy(
            src_ref=total,
            dst_ref=zparts.at[pl.ds(pl.multiple_of(z * CH, CH), CH)],
            send_sem=z_send.at[step], recv_sem=z_recv.at[step],
            device_id=layer_dev((z + step) % LAYERS), device_id_type=MESH,
        )

    for step in range(1, LAYERS):
        @pl.when(z + step < LAYERS)
        def _(step=step):
            z_copy(step).start()

    def group(b, n):
        src = parts if b == 0 else tree
        return src.at[pl.ds(pl.multiple_of((base[b] + n) * CH, CH), CH)]

    def share(b, src, mm):
        return pltpu.make_async_remote_copy(
            src_ref=src, dst_ref=left.at[b, pl.ds(my_row, CH)],
            send_sem=lv_send.at[b], recv_sem=lv_recv.at[b],
            device_id=plane_dev(mm), device_id_type=MESH,
        )

    for b in range(PLANE_BITS):
        def send_left(n, _, b=b):
            low = n % 2**b
            high = n // 2**b
            mm = high * 2 ** (b + 1) + 2**b + low

            @pl.when(mm != m)
            def _():
                share(b, group(b, 2 * high), mm).start()

            @pl.when(mm == m)
            def _():
                left[b, pl.ds(my_row, CH), :] = group(b, 2 * high)[...]

            return 0

        lax.fori_loop(0, PLANE // 2, send_left, 0)

    bits = [(m // 2**b) % 2 for b in range(PLANE_BITS)] + [(z // 2**b) % 2 for b in range(LAYER_BITS)]

    for b in range(PLANE_BITS + LAYER_BITS):
        @pl.when(bits[b] == 1)
        def _(b=b):
            for h in range(HEADS):
                w = lam[:, (3 + b) * HEADS + h : (3 + b) * HEADS + h + 1]
                scaled[b, :, head(h)] = (q[:, head(h)].astype(F32) * w).astype(BF16)

    for b in range(LAYER_BITS):
        lv = PLANE_BITS + b

        @pl.when(bits[lv] == 1)
        def _(b=b, lv=lv):
            first = (z // 2 ** (b + 1)) * 2 ** (b + 1)
            value = None
            for n in range(2**b):
                zz = first + n
                for step in range(1, LAYERS):
                    @pl.when(z - zz == step)
                    def _(step=step):
                        z_copy(step).wait_recv()
                got = zparts[pl.ds(pl.multiple_of(zz * CH, CH), CH), :]
                value = got if value is None else value + got
            ztree[b] = value
            left[lv, pl.ds(my_row, CH), :] = value

            def send_layer(j, _):
                share(lv, ztree.at[b], (m + j) % PLANE).start()
                return 0

            lax.fori_loop(1, PLANE, send_layer, 0)

    def level_wait(b, count, send):
        c = pltpu.make_async_remote_copy(
            src_ref=left.at[b, pl.ds(0, count * CH)], dst_ref=left.at[b, pl.ds(0, count * CH)],
            send_sem=lv_send.at[b], recv_sem=lv_recv.at[b],
            device_id=plane_dev((m + 1) % PLANE), device_id_type=MESH,
        )
        c.wait_send() if send else c.wait_recv()

    for b in range(PLANE_BITS + LAYER_BITS):
        @pl.when(bits[b] == 1)
        def _(b=b):
            level_wait(b, PLANE - 1, False)
            for h in range(HEADS):
                acc[:, head(h)] += jnp.dot(
                    scaled[b, :, head(h)], left[b, head(h), :].astype(BF16), preferred_element_type=F32
                )

    for h in range(HEADS):
        x = acc[:, head(h)]
        square = jnp.mean(x * x, axis=-1, keepdims=True)
        o_ref[:, head(h)] = (x * lax.rsqrt(square + EPS)).astype(BF16)

    plane_wait(True)
    for step in range(1, LAYERS):
        @pl.when(z + step < LAYERS)
        def _(step=step):
            z_copy(step).wait_send()
    for b in range(PLANE_BITS):
        for bit in range(2):
            @pl.when(bits[b] == bit)
            def _(b=b, bit=bit):
                level_wait(b, PLANE // 2 - bit, True)
    for b in range(PLANE_BITS, PLANE_BITS + LAYER_BITS):
        @pl.when(bits[b] == 1)
        def _(b=b):
            level_wait(b, PLANE - 1, True)


def on_device(query_rows, key_rows, value_rows, level_ids, level_table):
    hbm = pl.BlockSpec(memory_space=pl.ANY)
    vmem = pl.BlockSpec(memory_space=pltpu.VMEM)
    dma = pltpu.SemaphoreType.DMA
    all_levels = PLANE_BITS + LAYER_BITS
    return pl.pallas_call(
        kernel,
        out_shape=jax.ShapeDtypeStruct((TOK, HEADS * HD), BF16),
        in_specs=[hbm, hbm, hbm, vmem, vmem],
        out_specs=vmem,
        scratch_shapes=[
            pltpu.VMEM((TOK, HEADS * HD), BF16),
            pltpu.VMEM((TOK, HEADS * HD), BF16),
            pltpu.VMEM((TOK, HEADS * HD), BF16),
            pltpu.VMEM((ROWS, HD), F32),
            pltpu.VMEM((PLANE * CH, HD), F32),
            pltpu.VMEM((PLANE * CH, HD), F32),
            pltpu.VMEM((LAYERS * CH, HD), F32),
            pltpu.VMEM((LAYER_BITS, CH, HD), F32),
            pltpu.VMEM((all_levels, ROWS, HD), F32),
            pltpu.VMEM((TOK, LEVELS * HEADS), F32),
            pltpu.VMEM((TOK, HEADS * HD), F32),
            pltpu.VMEM((all_levels, TOK, HEADS * HD), BF16),
            dma((3,)), dma, dma, dma((all_levels,)), dma((all_levels,)), dma((LAYERS,)), dma((LAYERS,)),
        ],
        compiler_params=pltpu.CompilerParams(collective_id=0, has_side_effects=True),
        name="fenwick",
    )(
        query_rows, key_rows, value_rows,
        level_ids.reshape(SPANS, SPAN), level_table.reshape(CLASSES, LEVELS * HEADS),
    )


def solution(mesh):
    rows = P(("outer", "inner"), None)
    return jax.shard_map(
        on_device, mesh=mesh,
        in_specs=(rows, rows, rows, P(("outer", "inner")), P()),
        out_specs=rows, check_vma=False,
    )
```

```python
import jax
import jax.numpy as jnp
from jax import lax
from jax.experimental import pallas as pl
from jax.experimental.pallas import tpu as pltpu
from jax.sharding import PartitionSpec as P

HEADS = 4
HD = 128
SPAN = 128
LEVELS = 16
CLASSES = 16
TOK = 512
SPANS = TOK // SPAN
ROWS = HEADS * HD
CHIPS = 16
LAYERS = 8
CHUNKS = 2 * CHIPS
CH = ROWS // CHUNKS
PER_HEAD = CHUNKS // HEADS
EPS = 1e-06
MESH = pl.DeviceIdType.MESH
F32 = jnp.float32
BF16 = jnp.bfloat16

OFFSETS = sorted(
    ((dx, dy) for dx in range(4) for dy in range(4) if dx or dy),
    key=lambda o: -(min(o[0], 4 - o[0]) + min(o[1], 4 - o[1])),
)
STEPS = sorted(range(1, LAYERS), key=lambda s: -min(s, LAYERS - s))


def kernel(
    q_hbm, k_hbm, v_hbm, ids_hbm, table_hbm, o_ref,
    q, k, v, ids, table, state, parts, pack, total, zparts, zsum, zero, low, high, lam, acc, scaled,
    in_sem, rs_send, rs_recv, zero_sem, lo_send, lo_recv, hi_send, hi_recv, fw_send, fw_recv, z_send, z_recv,
):
    outer = lax.axis_index("outer")
    inner = lax.axis_index("inner")
    z, x = lax.div(outer, 4), lax.rem(outer, 4)
    y, c = lax.div(inner, 2), lax.rem(inner, 2)
    p = x * 4 + y
    m = p * 2 + c
    mine = c * CHIPS + p
    xs = [lax.rem(x + dx, 4) for dx in range(4)]
    ys = [lax.rem(y + dy, 4) for dy in range(4)]

    def device(xx, yy, cc):
        return {"outer": z * 4 + xx, "inner": yy * 2 + cc}

    sibling = device(x, y, 1 - c)

    def layer_device(step):
        return {"outer": lax.rem(z + step, LAYERS) * 4 + x, "inner": inner}

    loads = [
        pltpu.make_async_copy(src, dst, in_sem.at[n])
        for n, (src, dst) in enumerate(
            ((k_hbm, k), (v_hbm, v), (ids_hbm, ids), (table_hbm, table), (q_hbm, q))
        )
    ]
    for load in loads:
        load.start()

    barrier = pltpu.get_barrier_semaphore()

    def greet(dev):
        pl.semaphore_signal(barrier, inc=1, device_id=dev, device_id_type=MESH)

    for dx, dy in OFFSETS:
        for cc in range(2):
            greet(device(xs[dx], ys[dy], cc))
    for step in STEPS:
        greet(layer_device(step))
    greet(sibling)

    def head(h):
        return slice(h * HD, (h + 1) * HD)

    def head_chunks(h):
        return slice(h * PER_HEAD, (h + 1) * PER_HEAD)

    def contract_tokens(a, b):
        return lax.dot_general(a, b, (((0,), (0,)), ((), ())), preferred_element_type=F32)

    loads[0].wait()
    loads[1].wait()
    for h in range(HEADS):
        state[head_chunks(h)] = contract_tokens(k[:, head(h)], v[:, head(h)]).reshape(PER_HEAD, CH, HD)

    pl.semaphore_wait(barrier, CHUNKS - 1 + LAYERS - 1)

    def to_owner(xx, yy, cc):
        return pltpu.make_async_remote_copy(
            src_ref=state.at[cc * CHIPS + xx * 4 + yy], dst_ref=parts.at[m],
            send_sem=rs_send, recv_sem=rs_recv,
            device_id=device(xx, yy, cc), device_id_type=MESH,
        )

    for dx, dy in OFFSETS:
        for cc in range(2):
            to_owner(xs[dx], ys[dy], cc).start()
    to_owner(x, y, 1 - c).start()
    parts[m] = state[mine]

    def zero_copy():
        return pltpu.make_async_remote_copy(
            src_ref=state, dst_ref=zero, send_sem=zero_sem.at[0], recv_sem=zero_sem.at[1],
            device_id=sibling, device_id_type=MESH,
        )

    @pl.when(c == 0)
    def _():
        zero_copy().start()

    bits = (
        [c]
        + [lax.rem(lax.div(p, 2**b), 2) for b in range(4)]
        + [lax.rem(lax.div(z, 2**b), 2) for b in range(3)]
    )
    for load in loads[2:]:
        load.wait()
    classes = lax.broadcasted_iota(jnp.int32, (CLASSES, SPAN), 0)
    causal = lax.broadcasted_iota(jnp.int32, (SPAN, SPAN), 0) >= lax.broadcasted_iota(
        jnp.int32, (SPAN, SPAN), 1
    )
    span_rows = [slice(n * SPAN, (n + 1) * SPAN) for n in range(SPANS)]
    for n in range(SPANS):
        hot = (ids[n : n + 1, :] == classes).astype(F32)
        for h in range(HEADS):
            lam[span_rows[n], h * LEVELS : (h + 1) * LEVELS] = lax.dot_general(
                hot, table[:, h, :], (((0,), (0,)), ((), ())),
                precision=lax.Precision.HIGHEST, preferred_element_type=F32,
            )

    def weight(rows, level, h):
        n = h * LEVELS + level
        return lam[rows, n : n + 1]

    for h in range(HEADS):
        spans = [contract_tokens(k[span_rows[n], head(h)], v[span_rows[n], head(h)]) for n in range(3)]
        first = [None, spans[0].astype(BF16), None, spans[2].astype(BF16)]
        second = (spans[0] + spans[1]).astype(BF16)
        for n in range(SPANS):
            rows = span_rows[n]
            q_now = q[rows, head(h)]
            scores = lax.dot_general(
                q_now, k[rows, head(h)], (((1,), (1,)), ((), ())), preferred_element_type=F32
            )
            weighted = jnp.where(causal, scores * weight(rows, 0, h), 0.0).astype(BF16)
            out = jnp.dot(weighted, v[rows, head(h)], preferred_element_type=F32)
            if n % 2 == 1:
                out += weight(rows, 1, h) * jnp.dot(q_now, first[n], preferred_element_type=F32)
            if n >= 2:
                out += weight(rows, 2, h) * jnp.dot(q_now, second, preferred_element_type=F32)
            acc[rows, head(h)] = out

    def scale(b):
        @pl.when(bits[b] == 1)
        def _():
            for h in range(HEADS):
                scaled[b, :, head(h)] = (q[:, head(h)].astype(F32) * weight(slice(0, TOK), 3 + b, h)).astype(BF16)

    for b in range(SCALE_FIRST):
        scale(b)

    def bytes_of(n, send_sem, recv_sem):
        return pltpu.make_async_remote_copy(
            src_ref=parts.at[pl.ds(0, n)], dst_ref=parts.at[pl.ds(0, n)],
            send_sem=send_sem, recv_sem=recv_sem, device_id=sibling, device_id_type=MESH,
        )

    bytes_of(CHUNKS - 1, rs_send, rs_recv).wait_recv()
    groups = [[parts[n] for n in range(CHUNKS)]]
    for b in range(5):
        below = groups[-1]
        groups.append([below[2 * n] + below[2 * n + 1] for n in range(len(below) // 2)])
    total[...] = groups[5][0]

    def z_copy(step):
        return pltpu.make_async_remote_copy(
            src_ref=total, dst_ref=zparts.at[z],
            send_sem=z_send.at[step], recv_sem=z_recv.at[step],
            device_id=layer_device(step), device_id_type=MESH,
        )

    for step in STEPS:
        @pl.when(z + step < LAYERS)
        def _(step=step):
            z_copy(step).start()

    for chip in range(1, CHIPS):
        ones = [b for b in range(4) if chip >> b & 1]
        for slot, b in enumerate(ones):
            pack[chip, slot] = groups[b + 1][(chip >> b) - 1]
    count = bits[1] + bits[2] + bits[3] + bits[4]

    for dx, dy in OFFSETS:
        xx, yy = xs[dx], ys[dy]
        chip = xx * 4 + yy
        ones = lax.rem(xx, 2) + lax.div(xx, 2) + lax.rem(yy, 2) + lax.div(yy, 2)
        for n in range(1, 5):
            @pl.when(ones == n)
            def _(xx=xx, yy=yy, chip=chip, n=n):
                pltpu.make_async_remote_copy(
                    src_ref=pack.at[chip, pl.ds(0, n)], dst_ref=low.at[pl.ds(0, n), mine],
                    send_sem=lo_send, recv_sem=lo_recv,
                    device_id=device(xx, yy, c), device_id_type=MESH,
                ).start()
    for slot in range(4):
        @pl.when(slot < count)
        def _(slot=slot):
            low[slot, mine] = pack[p, slot]

    for b in range(SCALE_FIRST, 8):
        scale(b)

    def share(b, xx, yy, cc):
        return pltpu.make_async_remote_copy(
            src_ref=zsum.at[b], dst_ref=high.at[b, mine],
            send_sem=hi_send.at[b], recv_sem=hi_recv.at[b],
            device_id=device(xx, yy, cc), device_id_type=MESH,
        )

    direct = [False, False, LAST_DIRECT]
    for b in range(3):
        @pl.when(bits[5 + b] == 1)
        def _(b=b):
            first = lax.div(z, 2 ** (b + 1)) * 2 ** (b + 1)
            value = None
            for n in range(2**b):
                for step in range(1, LAYERS):
                    @pl.when(z - (first + n) == step)
                    def _(step=step):
                        z_copy(step).wait_recv()
                got = zparts[first + n]
                value = got if value is None else value + got
            zsum[b] = value
            for dx, dy in OFFSETS:
                share(b, xs[dx], ys[dy], c).start()
                if direct[b]:
                    share(b, xs[dx], ys[dy], 1 - c).start()
            if direct[b]:
                share(b, x, y, 1 - c).start()
            high[b, mine] = value

    half = pl.ds(c * CHIPS, CHIPS)

    def low_forward(n):
        return pltpu.make_async_remote_copy(
            src_ref=low.at[pl.ds(0, n), half], dst_ref=low.at[pl.ds(0, n), half],
            send_sem=fw_send.at[0], recv_sem=fw_recv.at[0], device_id=sibling, device_id_type=MESH,
        )

    def high_forward(b):
        return pltpu.make_async_remote_copy(
            src_ref=high.at[b, half], dst_ref=high.at[b, half],
            send_sem=fw_send.at[1 + b], recv_sem=fw_recv.at[1 + b], device_id=sibling, device_id_type=MESH,
        )

    def low_wait(n, send):
        copy = pltpu.make_async_remote_copy(
            src_ref=low.at[pl.ds(0, n), pl.ds(0, CHIPS - 1)], dst_ref=low.at[pl.ds(0, n), pl.ds(0, CHIPS - 1)],
            send_sem=lo_send, recv_sem=lo_recv, device_id=sibling, device_id_type=MESH,
        )
        copy.wait_send() if send else copy.wait_recv()

    def add(b, matrices):
        for h in range(HEADS):
            acc[:, head(h)] += jnp.dot(
                scaled[b, :, head(h)],
                matrices[head_chunks(h)].reshape(HD, HD).astype(BF16),
                preferred_element_type=F32,
            )

    for n in range(1, 5):
        @pl.when(count == n)
        def _(n=n):
            low_wait(n, False)
            low_forward(n).start()

    @pl.when(c == 1)
    def _():
        zero_copy().wait_recv()
        add(0, zero)

    for b in range(3):
        if not direct[b]:
            @pl.when(bits[5 + b] == 1)
            def _(b=b):
                bytes_of(CHIPS - 1, hi_send.at[b], hi_recv.at[b]).wait_recv()
                high_forward(b).start()

    for n in range(1, 5):
        @pl.when(count == n)
        def _(n=n):
            low_forward(n).wait_recv()
    slot = 0
    for b in range(1, 5):
        @pl.when(bits[b] == 1)
        def _(b=b, slot=slot):
            add(b, low.at[slot])
        slot = slot + bits[b]

    for b in range(3):
        @pl.when(bits[5 + b] == 1)
        def _(b=b):
            if direct[b]:
                bytes_of(CHUNKS - 1, hi_send.at[b], hi_recv.at[b]).wait_recv()
            else:
                high_forward(b).wait_recv()
            add(5 + b, high.at[b])

    for h in range(HEADS):
        value = acc[:, head(h)]
        square = jnp.mean(value * value, axis=-1, keepdims=True)
        o_ref[:, head(h)] = (value * lax.rsqrt(square + EPS)).astype(BF16)

    bytes_of(CHUNKS - 1, rs_send, rs_recv).wait_send()

    @pl.when(c == 0)
    def _():
        zero_copy().wait_send()

    for step in STEPS:
        @pl.when(z + step < LAYERS)
        def _(step=step):
            z_copy(step).wait_send()
    for n in range(5):
        @pl.when(count == n)
        def _(n=n):
            bytes_of(CHUNKS - n, lo_send, lo_recv).wait_send()
            if n:
                low_forward(n).wait_send()
    for b in range(3):
        @pl.when(bits[5 + b] == 1)
        def _(b=b):
            if direct[b]:
                bytes_of(CHUNKS - 1, hi_send.at[b], hi_recv.at[b]).wait_send()
            else:
                bytes_of(CHIPS - 1, hi_send.at[b], hi_recv.at[b]).wait_send()
                high_forward(b).wait_send()


SCALE_FIRST = 4
LAST_DIRECT = False


def on_device(query_rows, key_rows, value_rows, level_ids, level_table):
    hbm = pl.BlockSpec(memory_space=pl.ANY)
    vmem = pl.BlockSpec(memory_space=pltpu.VMEM)
    dma = pltpu.SemaphoreType.DMA
    wide = (TOK, HEADS * HD)
    return pl.pallas_call(
        kernel,
        out_shape=jax.ShapeDtypeStruct(wide, BF16),
        in_specs=[hbm] * 5,
        out_specs=vmem,
        scratch_shapes=[
            pltpu.VMEM(wide, BF16),
            pltpu.VMEM(wide, BF16),
            pltpu.VMEM(wide, BF16),
            pltpu.VMEM((SPANS, SPAN), jnp.int32),
            pltpu.VMEM((CLASSES, HEADS, LEVELS), F32),
            pltpu.VMEM((CHUNKS, CH, HD), F32),
            pltpu.VMEM((CHUNKS, CH, HD), F32),
            pltpu.VMEM((CHIPS, 4, CH, HD), F32),
            pltpu.VMEM((CH, HD), F32),
            pltpu.VMEM((LAYERS, CH, HD), F32),
            pltpu.VMEM((3, CH, HD), F32),
            pltpu.VMEM((CHUNKS, CH, HD), F32),
            pltpu.VMEM((4, CHUNKS, CH, HD), F32),
            pltpu.VMEM((3, CHUNKS, CH, HD), F32),
            pltpu.VMEM((TOK, LEVELS * HEADS), F32),
            pltpu.VMEM(wide, F32),
            pltpu.VMEM((8, *wide), BF16),
            dma((5,)), dma, dma, dma((2,)), dma, dma, dma((3,)), dma((3,)), dma((4,)), dma((4,)),
            dma((LAYERS,)), dma((LAYERS,)),
        ],
        compiler_params=pltpu.CompilerParams(collective_id=0, has_side_effects=True),
        name="fenwick",
    )(
        query_rows, key_rows, value_rows,
        level_ids.reshape(SPANS, SPAN), jnp.transpose(level_table, (0, 2, 1)),
    )


def solution(mesh):
    rows = P(("outer", "inner"), None)
    return jax.shard_map(
        on_device, mesh=mesh,
        in_specs=(rows, rows, rows, P(("outer", "inner")), P()),
        out_specs=rows, check_vma=False,
    )
```

```python
import jax
import jax.numpy as jnp
from jax import lax
from jax.experimental import pallas as pl
from jax.experimental.pallas import tpu as pltpu
from jax.sharding import PartitionSpec as P

HEADS = 4
HD = 128
SPAN = 128
LEVELS = 16
CLASSES = 16
TOK = 512
SPANS = TOK // SPAN
ROWS = HEADS * HD
CHIPS = 16
LAYERS = 8
CHUNKS = 2 * CHIPS
CH = ROWS // CHUNKS
PER_HEAD = CHUNKS // HEADS
EPS = 1e-06
MESH = pl.DeviceIdType.MESH
F32 = jnp.float32
BF16 = jnp.bfloat16

OFFSETS = sorted(
    ((dx, dy) for dx in range(4) for dy in range(4) if dx or dy),
    key=lambda o: -(min(o[0], 4 - o[0]) + min(o[1], 4 - o[1])),
)
STEPS = sorted(range(1, LAYERS), key=lambda s: -min(s, LAYERS - s))


def kernel(
    q_hbm, k_hbm, v_hbm, ids_hbm, table_hbm, acc,
    q, k, v, ids, table, state, parts, pack, total, zparts, zsum, zero, low, high, lam, scaled,
    in_sem, rs_send, rs_recv, zero_sem, lo_send, lo_recv, hi_send, hi_recv, fw_send, fw_recv, z_send, z_recv, ready,
):
    outer = lax.axis_index("outer")
    inner = lax.axis_index("inner")
    z, x = lax.div(outer, 4), lax.rem(outer, 4)
    y, c = lax.div(inner, 2), lax.rem(inner, 2)
    p = x * 4 + y
    m = p * 2 + c
    mine = c * CHIPS + p
    xs = [lax.rem(x + dx, 4) for dx in range(4)]
    ys = [lax.rem(y + dy, 4) for dy in range(4)]

    def device(xx, yy, cc):
        return {"outer": z * 4 + xx, "inner": yy * 2 + cc}

    sibling = device(x, y, 1 - c)

    def layer_device(step):
        return {"outer": lax.rem(z + step, LAYERS) * 4 + x, "inner": inner}

    loads = [
        pltpu.make_async_copy(src, dst, in_sem.at[n])
        for n, (src, dst) in enumerate(
            ((k_hbm, k), (v_hbm, v), (ids_hbm, ids), (table_hbm, table), (q_hbm, q))
        )
    ]
    for load in loads:
        load.start()

    barrier = pltpu.get_barrier_semaphore()

    def greet(dev):
        pl.semaphore_signal(barrier, inc=1, device_id=dev, device_id_type=MESH)

    for dx, dy in OFFSETS:
        for cc in range(2):
            greet(device(xs[dx], ys[dy], cc))
    greet(sibling)
    for step in STEPS:
        @pl.when(z + step < LAYERS)
        def _(step=step):
            greet(layer_device(step))

    def head(h):
        return slice(h * HD, (h + 1) * HD)

    def head_chunks(h):
        return slice(h * PER_HEAD, (h + 1) * PER_HEAD)

    def contract_tokens(a, b):
        return lax.dot_general(a, b, (((0,), (0,)), ((), ())), preferred_element_type=F32)

    loads[0].wait()
    loads[1].wait()
    for h in range(HEADS):
        state[head_chunks(h)] = contract_tokens(k[:, head(h)], v[:, head(h)]).reshape(PER_HEAD, CH, HD)

    pl.semaphore_wait(barrier, CHUNKS - 1 + z)

    def to_owner(xx, yy, cc):
        return pltpu.make_async_remote_copy(
            src_ref=state.at[cc * CHIPS + xx * 4 + yy], dst_ref=parts.at[m],
            send_sem=rs_send, recv_sem=rs_recv,
            device_id=device(xx, yy, cc), device_id_type=MESH,
        )

    for dx, dy in OFFSETS:
        for cc in range(2):
            to_owner(xs[dx], ys[dy], cc).start()
    to_owner(x, y, 1 - c).start()
    parts[m] = state[mine]

    def below(step):
        return {"outer": lax.rem(z + LAYERS - step, LAYERS) * 4 + x, "inner": inner}

    for step in STEPS:
        @pl.when(step <= z)
        def _(step=step):
            pl.semaphore_signal(ready.at[step], inc=1, device_id=below(step), device_id_type=MESH)

    def zero_copy():
        return pltpu.make_async_remote_copy(
            src_ref=state, dst_ref=zero, send_sem=zero_sem.at[0], recv_sem=zero_sem.at[1],
            device_id=sibling, device_id_type=MESH,
        )

    @pl.when(c == 0)
    def _():
        zero_copy().start()

    bits = (
        [c]
        + [lax.rem(lax.div(p, 2**b), 2) for b in range(4)]
        + [lax.rem(lax.div(z, 2**b), 2) for b in range(3)]
    )
    for load in loads[2:]:
        load.wait()
    classes = lax.broadcasted_iota(jnp.int32, (CLASSES, SPAN), 0)
    causal = lax.broadcasted_iota(jnp.int32, (SPAN, SPAN), 0) >= lax.broadcasted_iota(
        jnp.int32, (SPAN, SPAN), 1
    )
    span_rows = [slice(n * SPAN, (n + 1) * SPAN) for n in range(SPANS)]
    for n in range(SPANS):
        hot = (ids[n : n + 1, :] == classes).astype(F32)
        for h in range(HEADS):
            lam[span_rows[n], h * LEVELS : (h + 1) * LEVELS] = lax.dot_general(
                hot, table[:, h, :], (((0,), (0,)), ((), ())),
                precision=lax.Precision.HIGHEST, preferred_element_type=F32,
            )

    def weight(rows, level, h):
        n = h * LEVELS + level
        return lam[rows, n : n + 1]

    for h in range(HEADS):
        spans = [contract_tokens(k[span_rows[n], head(h)], v[span_rows[n], head(h)]) for n in range(3)]
        first = [None, spans[0].astype(BF16), None, spans[2].astype(BF16)]
        second = (spans[0] + spans[1]).astype(BF16)
        for n in range(SPANS):
            rows = span_rows[n]
            q_now = q[rows, head(h)]
            scores = lax.dot_general(
                q_now, k[rows, head(h)], (((1,), (1,)), ((), ())), preferred_element_type=F32
            )
            weighted = jnp.where(causal, scores * weight(rows, 0, h), 0.0).astype(BF16)
            out = jnp.dot(weighted, v[rows, head(h)], preferred_element_type=F32)
            if n % 2 == 1:
                out += weight(rows, 1, h) * jnp.dot(q_now, first[n], preferred_element_type=F32)
            if n >= 2:
                out += weight(rows, 2, h) * jnp.dot(q_now, second, preferred_element_type=F32)
            acc[rows, head(h)] = out

    def scale(b):
        @pl.when(bits[b] == 1)
        def _():
            for h in range(HEADS):
                scaled[b, :, head(h)] = (q[:, head(h)].astype(F32) * weight(slice(0, TOK), 3 + b, h)).astype(BF16)

    for b in range(SCALE_FIRST):
        scale(b)

    def bytes_of(n, send_sem, recv_sem):
        return pltpu.make_async_remote_copy(
            src_ref=parts.at[pl.ds(0, n)], dst_ref=parts.at[pl.ds(0, n)],
            send_sem=send_sem, recv_sem=recv_sem, device_id=sibling, device_id_type=MESH,
        )

    bytes_of(CHUNKS - 1, rs_send, rs_recv).wait_recv()
    groups = [[parts[n] for n in range(CHUNKS)]]
    for b in range(5):
        below = groups[-1]
        groups.append([below[2 * n] + below[2 * n + 1] for n in range(len(below) // 2)])
    total[...] = groups[5][0]

    def z_copy(step):
        return pltpu.make_async_remote_copy(
            src_ref=total, dst_ref=zparts.at[z],
            send_sem=z_send.at[step], recv_sem=z_recv.at[step],
            device_id=layer_device(step), device_id_type=MESH,
        )

    for step in STEPS:
        @pl.when(z + step < LAYERS)
        def _(step=step):
            pl.semaphore_wait(ready.at[step], 1)
            z_copy(step).start()

    for chip in range(1, CHIPS):
        ones = [b for b in range(4) if chip >> b & 1]
        for slot, b in enumerate(ones):
            pack[chip, slot] = groups[b + 1][(chip >> b) - 1]
    count = bits[1] + bits[2] + bits[3] + bits[4]

    for dx, dy in OFFSETS:
        xx, yy = xs[dx], ys[dy]
        chip = xx * 4 + yy
        ones = lax.rem(xx, 2) + lax.div(xx, 2) + lax.rem(yy, 2) + lax.div(yy, 2)
        for n in range(1, 5):
            @pl.when(ones == n)
            def _(xx=xx, yy=yy, chip=chip, n=n):
                pltpu.make_async_remote_copy(
                    src_ref=pack.at[chip, pl.ds(0, n)], dst_ref=low.at[pl.ds(0, n), mine],
                    send_sem=lo_send, recv_sem=lo_recv,
                    device_id=device(xx, yy, c), device_id_type=MESH,
                ).start()
    for slot in range(4):
        @pl.when(slot < count)
        def _(slot=slot):
            low[slot, mine] = pack[p, slot]

    for b in range(SCALE_FIRST, 8):
        scale(b)

    def share(b, xx, yy, cc):
        return pltpu.make_async_remote_copy(
            src_ref=zsum.at[b], dst_ref=high.at[b, mine],
            send_sem=hi_send.at[b], recv_sem=hi_recv.at[b],
            device_id=device(xx, yy, cc), device_id_type=MESH,
        )

    direct = [False, False, LAST_DIRECT]
    for b in HIGH_ORDER:
        @pl.when(bits[5 + b] == 1)
        def _(b=b):
            first = lax.div(z, 2 ** (b + 1)) * 2 ** (b + 1)
            value = None
            for n in range(2**b):
                for step in range(1, LAYERS):
                    @pl.when(z - (first + n) == step)
                    def _(step=step):
                        z_copy(step).wait_recv()
                got = zparts[first + n]
                value = got if value is None else value + got
            zsum[b] = value
            for dx, dy in OFFSETS:
                share(b, xs[dx], ys[dy], c).start()
                if direct[b]:
                    share(b, xs[dx], ys[dy], 1 - c).start()
            if direct[b]:
                share(b, x, y, 1 - c).start()
            high[b, mine] = value

    half = pl.ds(c * CHIPS, CHIPS)

    def low_forward(n):
        return pltpu.make_async_remote_copy(
            src_ref=low.at[pl.ds(0, n), half], dst_ref=low.at[pl.ds(0, n), half],
            send_sem=fw_send.at[0], recv_sem=fw_recv.at[0], device_id=sibling, device_id_type=MESH,
        )

    def high_forward(b):
        return pltpu.make_async_remote_copy(
            src_ref=high.at[b, half], dst_ref=high.at[b, half],
            send_sem=fw_send.at[1 + b], recv_sem=fw_recv.at[1 + b], device_id=sibling, device_id_type=MESH,
        )

    def low_wait(n, send):
        copy = pltpu.make_async_remote_copy(
            src_ref=low.at[pl.ds(0, n), pl.ds(0, CHIPS - 1)], dst_ref=low.at[pl.ds(0, n), pl.ds(0, CHIPS - 1)],
            send_sem=lo_send, recv_sem=lo_recv, device_id=sibling, device_id_type=MESH,
        )
        copy.wait_send() if send else copy.wait_recv()

    def add(b, matrices):
        for h in range(HEADS):
            acc[:, head(h)] += jnp.dot(
                scaled[b, :, head(h)],
                matrices[head_chunks(h)].reshape(HD, HD).astype(BF16),
                preferred_element_type=F32,
            )

    for n in range(1, 5):
        @pl.when(count == n)
        def _(n=n):
            low_wait(n, False)
            low_forward(n).start()

    @pl.when(c == 1)
    def _():
        zero_copy().wait_recv()
        add(0, zero)

    for b in range(3):
        if not direct[b]:
            @pl.when(bits[5 + b] == 1)
            def _(b=b):
                bytes_of(CHIPS - 1, hi_send.at[b], hi_recv.at[b]).wait_recv()
                high_forward(b).start()

    for n in range(1, 5):
        @pl.when(count == n)
        def _(n=n):
            low_forward(n).wait_recv()
    slot = 0
    for b in range(1, 5):
        @pl.when(bits[b] == 1)
        def _(b=b, slot=slot):
            add(b, low.at[slot])
        slot = slot + bits[b]

    for b in range(3):
        @pl.when(bits[5 + b] == 1)
        def _(b=b):
            if direct[b]:
                bytes_of(CHUNKS - 1, hi_send.at[b], hi_recv.at[b]).wait_recv()
            else:
                high_forward(b).wait_recv()
            add(5 + b, high.at[b])

    bytes_of(CHUNKS - 1, rs_send, rs_recv).wait_send()

    @pl.when(c == 0)
    def _():
        zero_copy().wait_send()

    for step in STEPS:
        @pl.when(z + step < LAYERS)
        def _(step=step):
            z_copy(step).wait_send()
    for n in range(5):
        @pl.when(count == n)
        def _(n=n):
            bytes_of(CHUNKS - n, lo_send, lo_recv).wait_send()
            if n:
                low_forward(n).wait_send()
    for b in range(3):
        @pl.when(bits[5 + b] == 1)
        def _(b=b):
            if direct[b]:
                bytes_of(CHUNKS - 1, hi_send.at[b], hi_recv.at[b]).wait_send()
            else:
                bytes_of(CHIPS - 1, hi_send.at[b], hi_recv.at[b]).wait_send()
                high_forward(b).wait_send()


SCALE_FIRST = 4
HIGH_ORDER = (2, 0, 1)
LAST_DIRECT = False


def normalize(x_ref, o_ref):
    for h in range(HEADS):
        cols = slice(h * HD, (h + 1) * HD)
        value = x_ref[:, cols]
        square = jnp.mean(value * value, axis=-1, keepdims=True)
        o_ref[:, cols] = (value * lax.rsqrt(square + EPS)).astype(BF16)


def on_device(query_rows, key_rows, value_rows, level_ids, level_table):
    hbm = pl.BlockSpec(memory_space=pltpu.HBM)
    vmem = pl.BlockSpec(memory_space=pltpu.VMEM)
    dma = pltpu.SemaphoreType.DMA
    wide = (TOK, HEADS * HD)
    unnormed = pl.pallas_call(
        kernel,
        out_shape=jax.ShapeDtypeStruct(wide, F32),
        in_specs=[hbm] * 5,
        out_specs=vmem,
        scratch_shapes=[
            pltpu.VMEM(wide, BF16),
            pltpu.VMEM(wide, BF16),
            pltpu.VMEM(wide, BF16),
            pltpu.VMEM((SPANS, SPAN), jnp.int32),
            pltpu.VMEM((CLASSES, HEADS, LEVELS), F32),
            pltpu.VMEM((CHUNKS, CH, HD), F32),
            pltpu.VMEM((CHUNKS, CH, HD), F32),
            pltpu.VMEM((CHIPS, 4, CH, HD), F32),
            pltpu.VMEM((CH, HD), F32),
            pltpu.VMEM((LAYERS, CH, HD), F32),
            pltpu.VMEM((3, CH, HD), F32),
            pltpu.VMEM((CHUNKS, CH, HD), F32),
            pltpu.VMEM((4, CHUNKS, CH, HD), F32),
            pltpu.VMEM((3, CHUNKS, CH, HD), F32),
            pltpu.VMEM((TOK, LEVELS * HEADS), F32),
            pltpu.VMEM((8, *wide), BF16),
            dma((5,)), dma, dma, dma((2,)), dma, dma, dma((3,)), dma((3,)), dma((4,)), dma((4,)),
            dma((LAYERS,)), dma((LAYERS,)), pltpu.SemaphoreType.REGULAR((LAYERS,)),
        ],
        compiler_params=pltpu.CompilerParams(collective_id=0, has_side_effects=True, vmem_limit_bytes=24 * 2**20),
        name="fenwick",
    )(
        *[
            pltpu.with_memory_space_constraint(a, pltpu.HBM)
            for a in (
                query_rows, key_rows, value_rows,
                level_ids.reshape(SPANS, SPAN), jnp.transpose(level_table, (0, 2, 1)),
            )
        ]
    )
    return pl.pallas_call(
        normalize,
        out_shape=jax.ShapeDtypeStruct(wide, BF16),
        in_specs=[vmem],
        out_specs=vmem,
        compiler_params=pltpu.CompilerParams(vmem_limit_bytes=8 * 2**20),
        name="normalize",
    )(unnormed)


def solution(mesh):
    rows = P(("outer", "inner"), None)
    return jax.shard_map(
        on_device, mesh=mesh,
        in_specs=(rows, rows, rows, P(("outer", "inner")), P()),
        out_specs=rows, check_vma=False,
    )
```

```python
import jax
import jax.numpy as jnp
from jax import lax
from jax.experimental import pallas as pl
from jax.experimental.pallas import tpu as pltpu
from jax.sharding import PartitionSpec as P

HEADS = 4
HD = 128
SPAN = 128
LEVELS = 16
CLASSES = 16
TOK = 512
SPANS = TOK // SPAN
CHIPS = 16
LAYERS = 8
CHUNKS = 2 * CHIPS
CH = HEADS * HD // CHUNKS
PER_HEAD = CHUNKS // HEADS
HALF = HEADS * HD // 2
EPS = 1e-06
MESH = pl.DeviceIdType.MESH
F32 = jnp.float32
BF16 = jnp.bfloat16

OFFSETS = sorted(
    ((dx, dy) for dx in range(4) for dy in range(4) if dx or dy),
    key=lambda o: -(min(o[0], 4 - o[0]) + min(o[1], 4 - o[1])),
)
STEPS = sorted(range(1, LAYERS), key=lambda s: -min(s, LAYERS - s))
SCALE_FIRST = 4
HIGH_ORDER = (0, 2, 1)
Y_EARLY = True


def kernel(
    q_hbm, k_hbm, v_hbm, ids_hbm, table_hbm, acc,
    q, k, v, ids, table, state, other, chip_state, parts, sums, total, five, six, zparts, zsum, zero, pair, low, high,
    lam, scaled,
    in_sem, other_sem, rs_send, rs_recv, zero_sem, y_send, y_recv, lo_send, lo_recv, hi_send, hi_recv, fw_send, fw_recv,
    z_send, z_recv, five_send, five_recv, six_send, six_recv, ready,
):
    outer = lax.axis_index("outer")
    inner = lax.axis_index("inner")
    z, x = lax.div(outer, 4), lax.rem(outer, 4)
    y, c = lax.div(inner, 2), lax.rem(inner, 2)
    p = x * 4 + y
    place = lax.rem(z, 4)
    mine = c * CHIPS + p
    xs = [lax.rem(x + dx, 4) for dx in range(4)]
    ys = [lax.rem(y + dy, 4) for dy in range(4)]

    def device(xx, yy, cc, layer=None):
        return {"outer": (z if layer is None else layer) * 4 + xx, "inner": yy * 2 + cc}

    sibling = device(x, y, 1 - c)

    def in_layer(layer):
        return {"outer": layer * 4 + x, "inner": inner}

    def columns(cc):
        return pl.ds(pl.multiple_of(cc * HALF, HALF), HALF)

    def load(src, dst, n):
        return pltpu.make_async_copy(src, dst, in_sem.at[n])

    key_loads = [
        [
            load(src.at[:, columns(cc)], dst.at[:, columns(cc)], 2 * n + i)
            for i, (src, dst) in enumerate(((k_hbm, k), (v_hbm, v)))
        ]
        for n, cc in enumerate((1 - c, c))
    ]
    late_loads = [load(ids_hbm, ids, 4), load(table_hbm, table, 5), load(q_hbm, q, 6)]
    for copy in key_loads[0] + key_loads[1] + late_loads:
        copy.start()

    barrier = pltpu.get_barrier_semaphore()

    def greet(dev):
        pl.semaphore_signal(barrier, inc=1, device_id=dev, device_id_type=MESH)

    for dx, dy in OFFSETS:
        greet(device(xs[dx], ys[dy], c))
    greet(sibling)
    for step in STEPS:
        @pl.when(z + step < LAYERS)
        def _(step=step):
            greet(in_layer(z + step))

    def head(h):
        return slice(h * HD, (h + 1) * HD)

    def head_chunks(h):
        return slice(h * PER_HEAD, (h + 1) * PER_HEAD)

    def contract_tokens(a, b):
        return lax.dot_general(a, b, (((0,), (0,)), ((), ())), preferred_element_type=F32)

    def half_state(n, cc):
        for copy in key_loads[n]:
            copy.wait()
        for i in range(HEADS // 2):
            cols = pl.ds(pl.multiple_of(cc * HALF + i * HD, HD), HD)
            value = contract_tokens(k[:, cols], v[:, cols])
            state[pl.ds(cc * CHIPS + i * PER_HEAD, PER_HEAD)] = value.reshape(PER_HEAD, CH, HD)

    half_state(0, 1 - c)
    pl.semaphore_wait(barrier, CHIPS - 1 + 1 + z)
    half, other_half = pl.ds(c * CHIPS, CHIPS), pl.ds((1 - c) * CHIPS, CHIPS)
    other_copy = pltpu.make_async_remote_copy(
        src_ref=state.at[other_half], dst_ref=other,
        send_sem=other_sem.at[0], recv_sem=other_sem.at[1], device_id=sibling, device_id_type=MESH,
    )
    other_copy.start()
    half_state(1, c)

    for step in STEPS:
        @pl.when(step <= z)
        def _(step=step):
            pl.semaphore_signal(ready.at[step], inc=1, device_id=in_layer(z - step), device_id_type=MESH)

    other_copy.wait_recv()
    chip_state[...] = state[half] + other[...]

    def to_owner(xx, yy):
        return pltpu.make_async_remote_copy(
            src_ref=chip_state.at[xx * 4 + yy], dst_ref=parts.at[p],
            send_sem=rs_send, recv_sem=rs_recv,
            device_id=device(xx, yy, c), device_id_type=MESH,
        )

    for dx, dy in OFFSETS:
        to_owner(xs[dx], ys[dy]).start()
    parts[p] = chip_state[p]

    straight = ((0, 3, 1), (1, 3, 2), (0, 2, 1), (1, 2, 2), (0, 1, 0), (2, 3, 0))

    def straight_copy(to, slot):
        dst = low.at[0, half] if slot == 0 else pair.at[slot - 1]
        return pltpu.make_async_remote_copy(
            src_ref=chip_state, dst_ref=dst,
            send_sem=y_send.at[to], recv_sem=y_recv.at[slot],
            device_id=device(x, to, c), device_id_type=MESH,
        )

    def start_straight():
        for at, to, slot in straight:
            @pl.when(y == at)
            def _(to=to, slot=slot):
                straight_copy(to, slot).start()

    if Y_EARLY:
        start_straight()

    zero_copy = pltpu.make_async_remote_copy(
        src_ref=state.at[pl.ds(0, CHIPS)], dst_ref=zero, send_sem=zero_sem.at[0], recv_sem=zero_sem.at[1],
        device_id=sibling, device_id_type=MESH,
    )

    @pl.when(c == 0)
    def _():
        zero_copy.start()

    bits = (
        [c]
        + [lax.rem(lax.div(p, 2**b), 2) for b in range(4)]
        + [lax.rem(lax.div(z, 2**b), 2) for b in range(3)]
    )
    for copy in late_loads:
        copy.wait()
    classes = lax.broadcasted_iota(jnp.int32, (CLASSES, SPAN), 0)
    causal = lax.broadcasted_iota(jnp.int32, (SPAN, SPAN), 0) >= lax.broadcasted_iota(
        jnp.int32, (SPAN, SPAN), 1
    )
    span_rows = [slice(n * SPAN, (n + 1) * SPAN) for n in range(SPANS)]
    for n in range(SPANS):
        hot = (ids[n : n + 1, :] == classes).astype(F32)
        for h in range(HEADS):
            lam[span_rows[n], h * LEVELS : (h + 1) * LEVELS] = lax.dot_general(
                hot, table[:, h, :], (((0,), (0,)), ((), ())),
                precision=lax.Precision.HIGHEST, preferred_element_type=F32,
            )

    def weight(rows, level, h):
        n = h * LEVELS + level
        return lam[rows, n : n + 1]

    for h in range(HEADS):
        spans = [contract_tokens(k[span_rows[n], head(h)], v[span_rows[n], head(h)]) for n in range(3)]
        first = [None, spans[0].astype(BF16), None, spans[2].astype(BF16)]
        second = (spans[0] + spans[1]).astype(BF16)
        for n in range(SPANS):
            rows = span_rows[n]
            q_now = q[rows, head(h)]
            scores = lax.dot_general(
                q_now, k[rows, head(h)], (((1,), (1,)), ((), ())), preferred_element_type=F32
            )
            weighted = jnp.where(causal, scores * weight(rows, 0, h), 0.0).astype(BF16)
            out = jnp.dot(weighted, v[rows, head(h)], preferred_element_type=F32)
            if n % 2 == 1:
                out += weight(rows, 1, h) * jnp.dot(q_now, first[n], preferred_element_type=F32)
            if n >= 2:
                out += weight(rows, 2, h) * jnp.dot(q_now, second, preferred_element_type=F32)
            acc[rows, head(h)] = out

    def scale(b):
        @pl.when(bits[b] == 1)
        def _():
            for h in range(HEADS):
                scaled[b, :, head(h)] = (q[:, head(h)].astype(F32) * weight(slice(0, TOK), 3 + b, h)).astype(BF16)

    for b in range(SCALE_FIRST):
        scale(b)

    def bytes_of(n, send_sem, recv_sem):
        return pltpu.make_async_remote_copy(
            src_ref=state.at[pl.ds(0, n)], dst_ref=state.at[pl.ds(0, n)],
            send_sem=send_sem, recv_sem=recv_sem, device_id=sibling, device_id_type=MESH,
        )

    bytes_of(CHIPS - 1, rs_send, rs_recv).wait_recv()
    groups = [[parts[n] for n in range(CHIPS)]]
    for b in range(4):
        below = groups[-1]
        groups.append([below[2 * n] + below[2 * n + 1] for n in range(len(below) // 2)])
    total[...] = groups[4][0]

    def six_copy(step):
        return pltpu.make_async_remote_copy(
            src_ref=total, dst_ref=six.at[place],
            send_sem=six_send.at[step - 1], recv_sem=six_recv.at[place],
            device_id=in_layer(z + step), device_id_type=MESH,
        )

    six_steps = [(3, 2), (2, 1)]
    for at, steps in enumerate(six_steps):
        @pl.when(place == at)
        def _(steps=steps):
            for step in steps:
                pl.semaphore_wait(ready.at[step], 1)
                six_copy(step).start()

    five_copy = pltpu.make_async_remote_copy(
        src_ref=total, dst_ref=five.at[0],
        send_sem=five_send, recv_sem=five_recv.at[0],
        device_id=in_layer(z + 1), device_id_type=MESH,
    )

    @pl.when(bits[5] == 0)
    def _():
        pl.semaphore_wait(ready.at[1], 1)
        five_copy.start()

    sums[0], sums[1], sums[2] = groups[2][0], groups[2][2], groups[3][0]

    def low_copy(level, xx, yy):
        src = sums.at[lax.div(xx, 2)] if level == 3 else sums.at[2]
        return pltpu.make_async_remote_copy(
            src_ref=src, dst_ref=low.at[level - 1, mine],
            send_sem=lo_send.at[level - 3], recv_sem=lo_recv.at[level - 3],
            device_id=device(xx, yy, c), device_id_type=MESH,
        )

    for dx, dy in OFFSETS:
        xx, yy = xs[dx], ys[dy]
        for level, bit in ((3, lax.rem(xx, 2)), (4, lax.div(xx, 2))):
            @pl.when(bit == 1)
            def _(level=level, xx=xx, yy=yy):
                low_copy(level, xx, yy).start()
    low[2, mine] = sums[lax.div(x, 2)]
    low[3, mine] = sums[2]

    if not Y_EARLY:
        start_straight()

    def z_copy(layer):
        return pltpu.make_async_remote_copy(
            src_ref=total, dst_ref=zparts.at[z],
            send_sem=z_send.at[layer - 4], recv_sem=z_recv.at[z],
            device_id=in_layer(layer), device_id_type=MESH,
        )

    @pl.when(z < 4)
    def _():
        for layer in (7, 6, 5, 4):
            pl.semaphore_wait(ready.at[layer - z], 1)
            z_copy(layer).start()

    for b in range(SCALE_FIRST, 8):
        scale(b)

    def arrived(dst, sem):
        pltpu.make_async_remote_copy(
            src_ref=total, dst_ref=dst, send_sem=sem, recv_sem=sem, device_id=sibling, device_id_type=MESH
        ).wait_recv()

    def share(b, xx, yy):
        return pltpu.make_async_remote_copy(
            src_ref=zsum.at[b], dst_ref=high.at[b, mine],
            send_sem=hi_send.at[b], recv_sem=hi_recv.at[b],
            device_id=device(xx, yy, c), device_id_type=MESH,
        )

    def spread(b, sources, sems):
        @pl.when(bits[5 + b] == 1)
        def _():
            count = sources.shape[0]
            for n in range(count):
                arrived(sources.at[n], sems.at[n])
            values = [sources[n] for n in range(count)]
            while len(values) > 1:
                values = [values[i] + values[i + 1] for i in range(0, len(values), 2)]
            zsum[b] = values[0]
            for dx, dy in OFFSETS:
                share(b, xs[dx], ys[dy]).start()
            high[b, mine] = values[0]

    sources = ((five, five_recv), (six, six_recv), (zparts, z_recv))
    for b in HIGH_ORDER:
        spread(b, *sources[b])

    def low_forward(b):
        return pltpu.make_async_remote_copy(
            src_ref=low.at[b - 1, half], dst_ref=low.at[b - 1, half],
            send_sem=fw_send.at[2 + b], recv_sem=fw_recv.at[2 + b], device_id=sibling, device_id_type=MESH,
        )

    def high_forward(b):
        return pltpu.make_async_remote_copy(
            src_ref=high.at[b, half], dst_ref=high.at[b, half],
            send_sem=fw_send.at[b], recv_sem=fw_recv.at[b], device_id=sibling, device_id_type=MESH,
        )

    def add(b, matrix):
        for h in range(HEADS):
            acc[:, head(h)] += jnp.dot(
                scaled[b, :, head(h)], matrix(h).reshape(HD, HD).astype(BF16), preferred_element_type=F32
            )

    def straight_wait(slot):
        bytes_of(CHIPS, y_send.at[0], y_recv.at[slot]).wait_recv()

    @pl.when(bits[1] == 1)
    def _():
        straight_wait(0)
        low_forward(1).start()

    @pl.when(bits[2] == 1)
    def _():
        straight_wait(1)
        straight_wait(2)
        low[1, half] = pair[0] + pair[1]
        low_forward(2).start()

    for b in (3, 4):
        @pl.when(bits[b] == 1)
        def _(b=b):
            bytes_of(CHIPS - 1, lo_send.at[b - 3], lo_recv.at[b - 3]).wait_recv()
            low_forward(b).start()

    def high_wait(b):
        @pl.when(bits[5 + b] == 1)
        def _():
            bytes_of(CHIPS - 1, hi_send.at[b], hi_recv.at[b]).wait_recv()
            high_forward(b).start()

    @pl.when(c == 1)
    def _():
        zero_copy.wait_recv()
        add(0, lambda h: (zero if h < 2 else other)[head_chunks(h % 2)])

    def add_low(b):
        @pl.when(bits[b] == 1)
        def _():
            low_forward(b).wait_recv()
            add(b, lambda h: low[b - 1, head_chunks(h)])

    add_low(1)
    add_low(2)
    high_wait(HIGH_ORDER[0])
    add_low(3)
    high_wait(HIGH_ORDER[1])
    add_low(4)
    high_wait(HIGH_ORDER[2])

    for b in HIGH_ORDER:
        @pl.when(bits[5 + b] == 1)
        def _(b=b):
            high_forward(b).wait_recv()
            add(5 + b, lambda h: high[b, head_chunks(h)])

    other_copy.wait_send()
    bytes_of(CHIPS - 1, rs_send, rs_recv).wait_send()

    @pl.when(c == 0)
    def _():
        zero_copy.wait_send()

    for at, steps in enumerate(six_steps):
        @pl.when(place == at)
        def _(steps=steps):
            for step in steps:
                six_copy(step).wait_send()

    @pl.when(bits[5] == 0)
    def _():
        five_copy.wait_send()

    @pl.when(z < 4)
    def _():
        for layer in range(4, 8):
            z_copy(layer).wait_send()

    for at, to, slot in straight:
        @pl.when(y == at)
        def _(to=to, slot=slot):
            straight_copy(to, slot).wait_send()

    for b in (3, 4):
        for bit in range(2):
            @pl.when(bits[b] == bit)
            def _(b=b, bit=bit):
                bytes_of(CHIPS // 2 - bit, lo_send.at[b - 3], lo_recv.at[b - 3]).wait_send()
    for b in range(1, 5):
        @pl.when(bits[b] == 1)
        def _(b=b):
            low_forward(b).wait_send()

    for b in range(3):
        @pl.when(bits[5 + b] == 1)
        def _(b=b):
            high_forward(b).wait_send()
            bytes_of(CHIPS - 1, hi_send.at[b], hi_recv.at[b]).wait_send()


def normalize(x_ref, o_hbm, out, sem):
    copies = []
    for n in range(SPANS):
        rows = slice(n * SPAN, (n + 1) * SPAN)
        for h in range(HEADS):
            cols = slice(h * HD, (h + 1) * HD)
            value = x_ref[rows, cols]
            square = jnp.mean(value * value, axis=-1, keepdims=True)
            out[rows, cols] = (value * lax.rsqrt(square + EPS)).astype(BF16)
        copies.append(pltpu.make_async_copy(out.at[rows], o_hbm.at[rows], sem.at[n]))
        copies[-1].start()
    for copy in copies:
        copy.wait()


def on_device(query_rows, key_rows, value_rows, level_ids, level_table):
    hbm = pl.BlockSpec(memory_space=pltpu.HBM)
    vmem = pl.BlockSpec(memory_space=pltpu.VMEM)
    dma = pltpu.SemaphoreType.DMA
    wide = (TOK, HEADS * HD)
    chunk = (CH, HD)
    unnormed = pl.pallas_call(
        kernel,
        out_shape=jax.ShapeDtypeStruct(wide, F32),
        in_specs=[hbm] * 5,
        out_specs=vmem,
        scratch_shapes=[
            pltpu.VMEM(wide, BF16),
            pltpu.VMEM(wide, BF16),
            pltpu.VMEM(wide, BF16),
            pltpu.VMEM((SPANS, SPAN), jnp.int32),
            pltpu.VMEM((CLASSES, HEADS, LEVELS), F32),
            pltpu.VMEM((CHUNKS, *chunk), F32),
            pltpu.VMEM((CHIPS, *chunk), F32),
            pltpu.VMEM((CHIPS, *chunk), F32),
            pltpu.VMEM((CHIPS, *chunk), F32),
            pltpu.VMEM((3, *chunk), F32),
            pltpu.VMEM(chunk, F32),
            pltpu.VMEM((1, *chunk), F32),
            pltpu.VMEM((2, *chunk), F32),
            pltpu.VMEM((4, *chunk), F32),
            pltpu.VMEM((3, *chunk), F32),
            pltpu.VMEM((CHIPS, *chunk), F32),
            pltpu.VMEM((2, CHIPS, *chunk), F32),
            pltpu.VMEM((4, CHUNKS, *chunk), F32),
            pltpu.VMEM((3, CHUNKS, *chunk), F32),
            pltpu.VMEM((TOK, LEVELS * HEADS), F32),
            pltpu.VMEM((8, *wide), BF16),
            dma((7,)), dma((2,)), dma, dma, dma((2,)), dma((4,)), dma((3,)), dma((2,)), dma((2,)), dma((3,)), dma((3,)),
            dma((7,)), dma((7,)),
            dma((4,)), dma((4,)), dma, dma((1,)), dma((3,)), dma((2,)), pltpu.SemaphoreType.REGULAR((LAYERS,)),
        ],
        compiler_params=pltpu.CompilerParams(
            collective_id=0, has_side_effects=True, vmem_limit_bytes=24 * 2**20
        ),
        name="fenwick",
    )(
        *[
            pltpu.with_memory_space_constraint(a, pltpu.HBM)
            for a in (
                query_rows, key_rows, value_rows,
                level_ids.reshape(SPANS, SPAN), jnp.transpose(level_table, (0, 2, 1)),
            )
        ]
    )
    return pl.pallas_call(
        normalize,
        out_shape=jax.ShapeDtypeStruct(wide, BF16),
        in_specs=[vmem],
        out_specs=hbm,
        scratch_shapes=[pltpu.VMEM(wide, BF16), dma((SPANS,))],
        compiler_params=pltpu.CompilerParams(vmem_limit_bytes=8 * 2**20),
        name="normalize",
    )(unnormed)


def solution(mesh):
    rows = P(("outer", "inner"), None)
    return jax.shard_map(
        on_device, mesh=mesh,
        in_specs=(rows, rows, rows, P(("outer", "inner")), P()),
        out_specs=rows, check_vma=False,
    )
```

```python
import jax
import jax.numpy as jnp
from jax import lax
from jax.experimental import pallas as pl
from jax.experimental.pallas import tpu as pltpu
from jax.sharding import PartitionSpec as P

HEADS = 4
HD = 128
SPAN = 128
LEVELS = 16
CLASSES = 16
TOK = 512
SPANS = TOK // SPAN
CHIPS = 16
LAYERS = 8
CHUNKS = 2 * CHIPS
CH = HEADS * HD // CHUNKS
PER_HEAD = CHUNKS // HEADS
HALF = HEADS * HD // 2
EPS = 1e-06
MESH = pl.DeviceIdType.MESH
F32 = jnp.float32
BF16 = jnp.bfloat16

OFFSETS = sorted(
    ((dx, dy) for dx in range(4) for dy in range(4) if dx or dy),
    key=lambda o: -(min(o[0], 4 - o[0]) + min(o[1], 4 - o[1])),
)
STEPS = sorted(range(1, LAYERS), key=lambda s: -min(s, LAYERS - s))
SCALE_FIRST = 6
HIGH_ORDER = (0, 2, 1)


def kernel(
    q_hbm, k_hbm, v_hbm, ids_hbm, table_hbm, acc,
    q, k, v, ids, table, state, other, chip_state, parts, sums, total, five, six, zparts, zsum, zero, low, high,
    lam, scaled,
    in_sem, other_sem, rs_send, rs_recv, zero_sem, y_send, y_recv, lo_send, lo_recv, hi_send, hi_recv, fw_send, fw_recv,
    z_send, z_recv, five_send, five_recv, six_send, six_recv, ready,
):
    outer = lax.axis_index("outer")
    inner = lax.axis_index("inner")
    z, x = lax.div(outer, 4), lax.rem(outer, 4)
    y, c = lax.div(inner, 2), lax.rem(inner, 2)
    p = x * 4 + y
    place = lax.rem(z, 4)
    mine = c * CHIPS + p
    xs = [lax.rem(x + dx, 4) for dx in range(4)]
    ys = [lax.rem(y + dy, 4) for dy in range(4)]

    def device(xx, yy, cc, layer=None):
        return {"outer": (z if layer is None else layer) * 4 + xx, "inner": yy * 2 + cc}

    sibling = device(x, y, 1 - c)

    def in_layer(layer):
        return {"outer": layer * 4 + x, "inner": inner}

    def columns(cc):
        return pl.ds(pl.multiple_of(cc * HALF, HALF), HALF)

    def load(src, dst, n):
        return pltpu.make_async_copy(src, dst, in_sem.at[n])

    key_loads = [
        [
            load(src.at[:, columns(cc)], dst.at[:, columns(cc)], 2 * n + i)
            for i, (src, dst) in enumerate(((k_hbm, k), (v_hbm, v)))
        ]
        for n, cc in enumerate((1 - c, c))
    ]
    late_loads = [load(ids_hbm, ids, 4), load(table_hbm, table, 5), load(q_hbm, q, 6)]
    for copy in key_loads[0] + key_loads[1] + late_loads:
        copy.start()

    barrier = pltpu.get_barrier_semaphore()

    def greet(dev):
        pl.semaphore_signal(barrier, inc=1, device_id=dev, device_id_type=MESH)

    for dx, dy in OFFSETS:
        greet(device(xs[dx], ys[dy], c))
    greet(sibling)
    for step in STEPS:
        @pl.when(z + step < LAYERS)
        def _(step=step):
            greet(in_layer(z + step))

    def head(h):
        return slice(h * HD, (h + 1) * HD)

    def head_chunks(h):
        return slice(h * PER_HEAD, (h + 1) * PER_HEAD)

    def contract_tokens(a, b):
        return lax.dot_general(a, b, (((0,), (0,)), ((), ())), preferred_element_type=F32)

    def half_state(n, cc):
        for copy in key_loads[n]:
            copy.wait()
        for i in range(HEADS // 2):
            cols = pl.ds(pl.multiple_of(cc * HALF + i * HD, HD), HD)
            value = contract_tokens(k[:, cols], v[:, cols])
            state[pl.ds(cc * CHIPS + i * PER_HEAD, PER_HEAD)] = value.reshape(PER_HEAD, CH, HD)

    half_state(0, 1 - c)
    pl.semaphore_wait(barrier, CHIPS - 1 + 1 + z)
    half, other_half = pl.ds(c * CHIPS, CHIPS), pl.ds((1 - c) * CHIPS, CHIPS)
    other_copy = pltpu.make_async_remote_copy(
        src_ref=state.at[other_half], dst_ref=other,
        send_sem=other_sem.at[0], recv_sem=other_sem.at[1], device_id=sibling, device_id_type=MESH,
    )
    other_copy.start()
    half_state(1, c)

    for step in STEPS:
        @pl.when(step <= z)
        def _(step=step):
            pl.semaphore_signal(ready.at[step], inc=1, device_id=in_layer(z - step), device_id_type=MESH)

    other_copy.wait_recv()
    chip_state[...] = state[half] + other[...]

    def to_owner(xx, yy):
        return pltpu.make_async_remote_copy(
            src_ref=chip_state.at[xx * 4 + yy], dst_ref=parts.at[p],
            send_sem=rs_send, recv_sem=rs_recv,
            device_id=device(xx, yy, c), device_id_type=MESH,
        )

    for dx, dy in OFFSETS:
        to_owner(xs[dx], ys[dy]).start()
    parts[p] = chip_state[p]

    bits = (
        [c]
        + [lax.rem(lax.div(p, 2**b), 2) for b in range(4)]
        + [lax.rem(lax.div(z, 2**b), 2) for b in range(3)]
    )
    near_copy = pltpu.make_async_remote_copy(
        src_ref=chip_state, dst_ref=low.at[0, half], send_sem=y_send, recv_sem=y_recv,
        device_id=device(x, lax.rem(y + 1, 4), c), device_id_type=MESH,
    )

    @pl.when(bits[1] == 0)
    def _():
        near_copy.start()

    zero_copy = pltpu.make_async_remote_copy(
        src_ref=state.at[pl.ds(0, CHIPS)], dst_ref=zero, send_sem=zero_sem.at[0], recv_sem=zero_sem.at[1],
        device_id=sibling, device_id_type=MESH,
    )

    @pl.when(c == 0)
    def _():
        zero_copy.start()

    for copy in late_loads:
        copy.wait()
    classes = lax.broadcasted_iota(jnp.int32, (CLASSES, SPAN), 0)
    causal = lax.broadcasted_iota(jnp.int32, (SPAN, SPAN), 0) >= lax.broadcasted_iota(
        jnp.int32, (SPAN, SPAN), 1
    )
    span_rows = [slice(n * SPAN, (n + 1) * SPAN) for n in range(SPANS)]
    for n in range(SPANS):
        hot = (ids[n : n + 1, :] == classes).astype(F32)
        for h in range(HEADS):
            lam[span_rows[n], h * LEVELS : (h + 1) * LEVELS] = lax.dot_general(
                hot, table[:, h, :], (((0,), (0,)), ((), ())),
                precision=lax.Precision.HIGHEST, preferred_element_type=F32,
            )

    def weight(rows, level, h):
        n = h * LEVELS + level
        return lam[rows, n : n + 1]

    for h in range(HEADS):
        spans = [contract_tokens(k[span_rows[n], head(h)], v[span_rows[n], head(h)]) for n in range(3)]
        first = [None, spans[0].astype(BF16), None, spans[2].astype(BF16)]
        second = (spans[0] + spans[1]).astype(BF16)
        for n in range(SPANS):
            rows = span_rows[n]
            q_now = q[rows, head(h)]
            scores = lax.dot_general(
                q_now, k[rows, head(h)], (((1,), (1,)), ((), ())), preferred_element_type=F32
            )
            weighted = jnp.where(causal, scores * weight(rows, 0, h), 0.0).astype(BF16)
            out = jnp.dot(weighted, v[rows, head(h)], preferred_element_type=F32)
            if n % 2 == 1:
                out += weight(rows, 1, h) * jnp.dot(q_now, first[n], preferred_element_type=F32)
            if n >= 2:
                out += weight(rows, 2, h) * jnp.dot(q_now, second, preferred_element_type=F32)
            acc[rows, head(h)] = out

    def scale(b):
        @pl.when(bits[b] == 1)
        def _():
            for h in range(HEADS):
                scaled[b, :, head(h)] = (q[:, head(h)].astype(F32) * weight(slice(0, TOK), 3 + b, h)).astype(BF16)

    for b in range(SCALE_FIRST):
        scale(b)

    def bytes_of(n, send_sem, recv_sem):
        return pltpu.make_async_remote_copy(
            src_ref=state.at[pl.ds(0, n)], dst_ref=state.at[pl.ds(0, n)],
            send_sem=send_sem, recv_sem=recv_sem, device_id=sibling, device_id_type=MESH,
        )

    bytes_of(CHIPS - 1, rs_send, rs_recv).wait_recv()
    groups = [[parts[n] for n in range(CHIPS)]]
    for b in range(4):
        below = groups[-1]
        groups.append([below[2 * n] + below[2 * n + 1] for n in range(len(below) // 2)])
    total[...] = groups[4][0]

    def six_copy(step):
        return pltpu.make_async_remote_copy(
            src_ref=total, dst_ref=six.at[place],
            send_sem=six_send.at[step - 1], recv_sem=six_recv.at[place],
            device_id=in_layer(z + step), device_id_type=MESH,
        )

    six_steps = [(3, 2), (2, 1)]
    for at, steps in enumerate(six_steps):
        @pl.when(place == at)
        def _(steps=steps):
            for step in steps:
                pl.semaphore_wait(ready.at[step], 1)
                six_copy(step).start()

    five_copy = pltpu.make_async_remote_copy(
        src_ref=total, dst_ref=five.at[0],
        send_sem=five_send, recv_sem=five_recv.at[0],
        device_id=in_layer(z + 1), device_id_type=MESH,
    )

    @pl.when(bits[5] == 0)
    def _():
        pl.semaphore_wait(ready.at[1], 1)
        five_copy.start()

    for n in range(4):
        sums[n] = groups[1][2 * n]
    sums[4], sums[5], sums[6] = groups[2][0], groups[2][2], groups[3][0]

    def low_source(level, xx):
        return {2: xx, 3: 4 + lax.div(xx, 2), 4: 6}[level]

    def low_copy(level, xx, yy):
        return pltpu.make_async_remote_copy(
            src_ref=sums.at[low_source(level, xx)], dst_ref=low.at[level - 1, mine],
            send_sem=lo_send.at[level - 2], recv_sem=lo_recv.at[level - 2],
            device_id=device(xx, yy, c), device_id_type=MESH,
        )

    for dx, dy in OFFSETS:
        xx, yy = xs[dx], ys[dy]
        for level, bit in ((2, lax.div(yy, 2)), (3, lax.rem(xx, 2)), (4, lax.div(xx, 2))):
            @pl.when(bit == 1)
            def _(level=level, xx=xx, yy=yy):
                low_copy(level, xx, yy).start()
    for level in (2, 3, 4):
        low[level - 1, mine] = sums[low_source(level, x)]

    def z_copy(layer):
        return pltpu.make_async_remote_copy(
            src_ref=total, dst_ref=zparts.at[z],
            send_sem=z_send.at[layer - 4], recv_sem=z_recv.at[z],
            device_id=in_layer(layer), device_id_type=MESH,
        )

    @pl.when(z < 4)
    def _():
        for layer in (7, 6, 5, 4):
            pl.semaphore_wait(ready.at[layer - z], 1)
            z_copy(layer).start()

    for b in range(SCALE_FIRST, 8):
        scale(b)

    def arrived(dst, sem):
        pltpu.make_async_remote_copy(
            src_ref=total, dst_ref=dst, send_sem=sem, recv_sem=sem, device_id=sibling, device_id_type=MESH
        ).wait_recv()

    def share(b, xx, yy):
        return pltpu.make_async_remote_copy(
            src_ref=zsum.at[b], dst_ref=high.at[b, mine],
            send_sem=hi_send.at[b], recv_sem=hi_recv.at[b],
            device_id=device(xx, yy, c), device_id_type=MESH,
        )

    def spread(b, sources, sems):
        @pl.when(bits[5 + b] == 1)
        def _():
            count = sources.shape[0]
            for n in range(count):
                arrived(sources.at[n], sems.at[n])
            values = [sources[n] for n in range(count)]
            while len(values) > 1:
                values = [values[i] + values[i + 1] for i in range(0, len(values), 2)]
            zsum[b] = values[0]
            for dx, dy in OFFSETS:
                share(b, xs[dx], ys[dy]).start()
            high[b, mine] = values[0]

    sources = ((five, five_recv), (six, six_recv), (zparts, z_recv))
    for b in HIGH_ORDER:
        spread(b, *sources[b])

    def low_forward(b):
        return pltpu.make_async_remote_copy(
            src_ref=low.at[b - 1, half], dst_ref=low.at[b - 1, half],
            send_sem=fw_send.at[2 + b], recv_sem=fw_recv.at[2 + b], device_id=sibling, device_id_type=MESH,
        )

    def high_forward(b):
        return pltpu.make_async_remote_copy(
            src_ref=high.at[b, half], dst_ref=high.at[b, half],
            send_sem=fw_send.at[b], recv_sem=fw_recv.at[b], device_id=sibling, device_id_type=MESH,
        )

    def add(b, matrix):
        for h in range(HEADS):
            acc[:, head(h)] += jnp.dot(
                scaled[b, :, head(h)], matrix(h).reshape(HD, HD).astype(BF16), preferred_element_type=F32
            )

    @pl.when(bits[1] == 1)
    def _():
        near_copy.wait_recv()
        low_forward(1).start()

    for b in (2, 3, 4):
        @pl.when(bits[b] == 1)
        def _(b=b):
            bytes_of(CHIPS - 1, lo_send.at[b - 2], lo_recv.at[b - 2]).wait_recv()
            low_forward(b).start()

    def high_wait(b):
        @pl.when(bits[5 + b] == 1)
        def _():
            bytes_of(CHIPS - 1, hi_send.at[b], hi_recv.at[b]).wait_recv()
            high_forward(b).start()

    @pl.when(c == 1)
    def _():
        zero_copy.wait_recv()
        add(0, lambda h: (zero if h < 2 else other)[head_chunks(h % 2)])

    def add_low(b):
        @pl.when(bits[b] == 1)
        def _():
            low_forward(b).wait_recv()
            add(b, lambda h: low[b - 1, head_chunks(h)])

    add_low(1)
    add_low(2)
    high_wait(HIGH_ORDER[0])
    add_low(3)
    high_wait(HIGH_ORDER[1])
    add_low(4)
    high_wait(HIGH_ORDER[2])

    for b in HIGH_ORDER:
        @pl.when(bits[5 + b] == 1)
        def _(b=b):
            high_forward(b).wait_recv()
            add(5 + b, lambda h: high[b, head_chunks(h)])

    other_copy.wait_send()
    bytes_of(CHIPS - 1, rs_send, rs_recv).wait_send()

    @pl.when(c == 0)
    def _():
        zero_copy.wait_send()

    for at, steps in enumerate(six_steps):
        @pl.when(place == at)
        def _(steps=steps):
            for step in steps:
                six_copy(step).wait_send()

    @pl.when(bits[5] == 0)
    def _():
        five_copy.wait_send()

    @pl.when(z < 4)
    def _():
        for layer in range(4, 8):
            z_copy(layer).wait_send()

    @pl.when(bits[1] == 0)
    def _():
        near_copy.wait_send()

    for b in (2, 3, 4):
        for bit in range(2):
            @pl.when(bits[b] == bit)
            def _(b=b, bit=bit):
                bytes_of(CHIPS // 2 - bit, lo_send.at[b - 2], lo_recv.at[b - 2]).wait_send()
    for b in range(1, 5):
        @pl.when(bits[b] == 1)
        def _(b=b):
            low_forward(b).wait_send()

    for b in range(3):
        @pl.when(bits[5 + b] == 1)
        def _(b=b):
            high_forward(b).wait_send()
            bytes_of(CHIPS - 1, hi_send.at[b], hi_recv.at[b]).wait_send()


def normalize(x_ref, o_hbm, out, sem):
    copies = []
    for n in range(SPANS):
        rows = slice(n * SPAN, (n + 1) * SPAN)
        for h in range(HEADS):
            cols = slice(h * HD, (h + 1) * HD)
            value = x_ref[rows, cols]
            square = jnp.mean(value * value, axis=-1, keepdims=True)
            out[rows, cols] = (value * lax.rsqrt(square + EPS)).astype(BF16)
        copies.append(pltpu.make_async_copy(out.at[rows], o_hbm.at[rows], sem.at[n]))
        copies[-1].start()
    for copy in copies:
        copy.wait()


def on_device(query_rows, key_rows, value_rows, level_ids, level_table):
    hbm = pl.BlockSpec(memory_space=pltpu.HBM)
    vmem = pl.BlockSpec(memory_space=pltpu.VMEM)
    dma = pltpu.SemaphoreType.DMA
    wide = (TOK, HEADS * HD)
    chunk = (CH, HD)
    unnormed = pl.pallas_call(
        kernel,
        out_shape=jax.ShapeDtypeStruct(wide, F32),
        in_specs=[hbm] * 5,
        out_specs=vmem,
        scratch_shapes=[
            pltpu.VMEM(wide, BF16),
            pltpu.VMEM(wide, BF16),
            pltpu.VMEM(wide, BF16),
            pltpu.VMEM((SPANS, SPAN), jnp.int32),
            pltpu.VMEM((CLASSES, HEADS, LEVELS), F32),
            pltpu.VMEM((CHUNKS, *chunk), F32),
            pltpu.VMEM((CHIPS, *chunk), F32),
            pltpu.VMEM((CHIPS, *chunk), F32),
            pltpu.VMEM((CHIPS, *chunk), F32),
            pltpu.VMEM((7, *chunk), F32),
            pltpu.VMEM(chunk, F32),
            pltpu.VMEM((1, *chunk), F32),
            pltpu.VMEM((2, *chunk), F32),
            pltpu.VMEM((4, *chunk), F32),
            pltpu.VMEM((3, *chunk), F32),
            pltpu.VMEM((CHIPS, *chunk), F32),
            pltpu.VMEM((4, CHUNKS, *chunk), F32),
            pltpu.VMEM((3, CHUNKS, *chunk), F32),
            pltpu.VMEM((TOK, LEVELS * HEADS), F32),
            pltpu.VMEM((8, *wide), BF16),
            dma((7,)), dma((2,)), dma, dma, dma((2,)), dma, dma, dma((3,)), dma((3,)), dma((3,)), dma((3,)),
            dma((7,)), dma((7,)),
            dma((4,)), dma((4,)), dma, dma((1,)), dma((3,)), dma((2,)), pltpu.SemaphoreType.REGULAR((LAYERS,)),
        ],
        compiler_params=pltpu.CompilerParams(
            collective_id=0, has_side_effects=True, vmem_limit_bytes=24 * 2**20
        ),
        name="fenwick",
    )(
        *[
            pltpu.with_memory_space_constraint(a, pltpu.HBM)
            for a in (
                query_rows, key_rows, value_rows,
                level_ids.reshape(SPANS, SPAN), jnp.transpose(level_table, (0, 2, 1)),
            )
        ]
    )
    return pl.pallas_call(
        normalize,
        out_shape=jax.ShapeDtypeStruct(wide, BF16),
        in_specs=[vmem],
        out_specs=hbm,
        scratch_shapes=[pltpu.VMEM(wide, BF16), dma((SPANS,))],
        compiler_params=pltpu.CompilerParams(vmem_limit_bytes=8 * 2**20),
        name="normalize",
    )(unnormed)


def solution(mesh):
    rows = P(("outer", "inner"), None)
    return jax.shard_map(
        on_device, mesh=mesh,
        in_specs=(rows, rows, rows, P(("outer", "inner")), P()),
        out_specs=rows, check_vma=False,
    )
```

```python
import jax
import jax.numpy as jnp
from jax import lax
from jax.experimental import pallas as pl
from jax.experimental.pallas import tpu as pltpu
from jax.sharding import PartitionSpec as P

HEADS = 4
HD = 128
SPAN = 128
LEVELS = 16
CLASSES = 16
TOK = 512
SPANS = TOK // SPAN
CHIPS = 16
LAYERS = 8
CHUNKS = 2 * CHIPS
CH = HEADS * HD // CHUNKS
PER_HEAD = CHUNKS // HEADS
HALF = HEADS * HD // 2
EPS = 1e-06
MESH = pl.DeviceIdType.MESH
F32 = jnp.float32
BF16 = jnp.bfloat16

OFFSETS = sorted(
    ((dx, dy) for dx in range(4) for dy in range(4) if dx or dy),
    key=lambda o: -(min(o[0], 4 - o[0]) + min(o[1], 4 - o[1])),
)
STEPS = sorted(range(1, LAYERS), key=lambda s: -min(s, LAYERS - s))
SCALE_FIRST = 6
HIGH_ORDER = (0, 2, 1)


def kernel(
    q_hbm, k_hbm, v_hbm, ids_hbm, table_hbm, acc,
    q, k, v, ids, table, state, other, chip_state, parts, sums, total, five, six, zparts, zsum, zero, low, high,
    lam, scaled,
    in_sem, other_sem, rs_send, rs_recv, zero_sem, y_send, y_recv, lo_send, lo_recv, hi_send, hi_recv, fw_send, fw_recv,
    z_send, z_recv, five_send, five_recv, six_send, six_recv, ready,
):
    outer = lax.axis_index("outer")
    inner = lax.axis_index("inner")
    z, x = lax.div(outer, 4), lax.rem(outer, 4)
    y, c = lax.div(inner, 2), lax.rem(inner, 2)
    p = x * 4 + y
    place = lax.rem(z, 4)
    mine = c * CHIPS + p
    xs = [lax.rem(x + dx, 4) for dx in range(4)]
    ys = [lax.rem(y + dy, 4) for dy in range(4)]

    def device(xx, yy, cc, layer=None):
        return {"outer": (z if layer is None else layer) * 4 + xx, "inner": yy * 2 + cc}

    sibling = device(x, y, 1 - c)

    def in_layer(layer):
        return {"outer": layer * 4 + x, "inner": inner}

    def columns(cc):
        return pl.ds(pl.multiple_of(cc * HALF, HALF), HALF)

    def load(src, dst, n):
        return pltpu.make_async_copy(src, dst, in_sem.at[n])

    key_loads = [
        [
            load(src.at[:, columns(cc)], dst.at[:, columns(cc)], 2 * n + i)
            for i, (src, dst) in enumerate(((k_hbm, k), (v_hbm, v)))
        ]
        for n, cc in enumerate((1 - c, c))
    ]
    late_loads = [load(ids_hbm, ids, 4), load(table_hbm, table, 5), load(q_hbm, q, 6)]
    for copy in key_loads[0]:
        copy.start()

    barrier = pltpu.get_barrier_semaphore()

    def greet(dev):
        pl.semaphore_signal(barrier, inc=1, device_id=dev, device_id_type=MESH)

    for dx, dy in OFFSETS:
        greet(device(xs[dx], ys[dy], c))
    greet(sibling)
    for step in STEPS:
        @pl.when(z + step < LAYERS)
        def _(step=step):
            greet(in_layer(z + step))

    def head(h):
        return slice(h * HD, (h + 1) * HD)

    def head_chunks(h):
        return slice(h * PER_HEAD, (h + 1) * PER_HEAD)

    def contract_tokens(a, b):
        return lax.dot_general(a, b, (((0,), (0,)), ((), ())), preferred_element_type=F32)

    def half_state(n, cc):
        for copy in key_loads[n]:
            copy.wait()
        for i in range(HEADS // 2):
            cols = pl.ds(pl.multiple_of(cc * HALF + i * HD, HD), HD)
            value = contract_tokens(k[:, cols], v[:, cols])
            state[pl.ds(cc * CHIPS + i * PER_HEAD, PER_HEAD)] = value.reshape(PER_HEAD, CH, HD)

    for copy in key_loads[1]:
        copy.start()
    half_state(0, 1 - c)
    pl.semaphore_wait(barrier, CHIPS - 1 + 1 + z)
    half, other_half = pl.ds(c * CHIPS, CHIPS), pl.ds((1 - c) * CHIPS, CHIPS)
    other_copy = pltpu.make_async_remote_copy(
        src_ref=state.at[other_half], dst_ref=other,
        send_sem=other_sem.at[0], recv_sem=other_sem.at[1], device_id=sibling, device_id_type=MESH,
    )
    other_copy.start()
    for copy in late_loads:
        copy.start()
    for step in STEPS:
        @pl.when(step <= z)
        def _(step=step):
            pl.semaphore_signal(ready.at[step], inc=1, device_id=in_layer(z - step), device_id_type=MESH)

    half_state(1, c)

    other_copy.wait_recv()
    chip_state[...] = state[half] + other[...]

    def to_owner(xx, yy):
        return pltpu.make_async_remote_copy(
            src_ref=chip_state.at[xx * 4 + yy], dst_ref=parts.at[p],
            send_sem=rs_send, recv_sem=rs_recv,
            device_id=device(xx, yy, c), device_id_type=MESH,
        )

    for dx, dy in OFFSETS:
        to_owner(xs[dx], ys[dy]).start()
    parts[p] = chip_state[p]

    bits = (
        [c]
        + [lax.rem(lax.div(p, 2**b), 2) for b in range(4)]
        + [lax.rem(lax.div(z, 2**b), 2) for b in range(3)]
    )
    near_copy = pltpu.make_async_remote_copy(
        src_ref=chip_state, dst_ref=low.at[0, half], send_sem=y_send, recv_sem=y_recv,
        device_id=device(x, lax.rem(y + 1, 4), c), device_id_type=MESH,
    )

    @pl.when(bits[1] == 0)
    def _():
        near_copy.start()

    zero_copy = pltpu.make_async_remote_copy(
        src_ref=state.at[pl.ds(0, CHIPS)], dst_ref=zero, send_sem=zero_sem.at[0], recv_sem=zero_sem.at[1],
        device_id=sibling, device_id_type=MESH,
    )

    @pl.when(c == 0)
    def _():
        zero_copy.start()

    for copy in late_loads:
        copy.wait()
    classes = lax.broadcasted_iota(jnp.int32, (CLASSES, SPAN), 0)
    causal = lax.broadcasted_iota(jnp.int32, (SPAN, SPAN), 0) >= lax.broadcasted_iota(
        jnp.int32, (SPAN, SPAN), 1
    )
    span_rows = [slice(n * SPAN, (n + 1) * SPAN) for n in range(SPANS)]
    for n in range(SPANS):
        hot = (ids[n : n + 1, :] == classes).astype(F32)
        for h in range(HEADS):
            lam[span_rows[n], h * LEVELS : (h + 1) * LEVELS] = lax.dot_general(
                hot, table[:, h, :], (((0,), (0,)), ((), ())),
                precision=lax.Precision.HIGHEST, preferred_element_type=F32,
            )

    def weight(rows, level, h):
        n = h * LEVELS + level
        return lam[rows, n : n + 1]

    for h in range(HEADS):
        spans = [contract_tokens(k[span_rows[n], head(h)], v[span_rows[n], head(h)]) for n in range(3)]
        first = [None, spans[0].astype(BF16), None, spans[2].astype(BF16)]
        second = (spans[0] + spans[1]).astype(BF16)
        for n in range(SPANS):
            rows = span_rows[n]
            q_now = q[rows, head(h)]
            scores = lax.dot_general(
                q_now, k[rows, head(h)], (((1,), (1,)), ((), ())), preferred_element_type=F32
            )
            weighted = jnp.where(causal, scores * weight(rows, 0, h), 0.0).astype(BF16)
            out = jnp.dot(weighted, v[rows, head(h)], preferred_element_type=F32)
            if n % 2 == 1:
                out += weight(rows, 1, h) * jnp.dot(q_now, first[n], preferred_element_type=F32)
            if n >= 2:
                out += weight(rows, 2, h) * jnp.dot(q_now, second, preferred_element_type=F32)
            acc[rows, head(h)] = out

    def scale(b):
        @pl.when(bits[b] == 1)
        def _():
            for h in range(HEADS):
                scaled[b, :, head(h)] = (q[:, head(h)].astype(F32) * weight(slice(0, TOK), 3 + b, h)).astype(BF16)

    for b in range(SCALE_FIRST):
        scale(b)

    def add(b, matrix):
        for h in range(HEADS):
            acc[:, head(h)] += jnp.dot(
                scaled[b, :, head(h)], matrix(h).reshape(HD, HD).astype(BF16), preferred_element_type=F32
            )

    @pl.when(c == 1)
    def _():
        zero_copy.wait_recv()
        add(0, lambda h: (zero if h < 2 else other)[head_chunks(h % 2)])

    def bytes_of(n, send_sem, recv_sem):
        return pltpu.make_async_remote_copy(
            src_ref=state.at[pl.ds(0, n)], dst_ref=state.at[pl.ds(0, n)],
            send_sem=send_sem, recv_sem=recv_sem, device_id=sibling, device_id_type=MESH,
        )

    bytes_of(CHIPS - 1, rs_send, rs_recv).wait_recv()
    groups = [[parts[n] for n in range(CHIPS)]]
    for b in range(4):
        below = groups[-1]
        groups.append([below[2 * n] + below[2 * n + 1] for n in range(len(below) // 2)])
    total[...] = groups[4][0]

    def six_copy(step):
        return pltpu.make_async_remote_copy(
            src_ref=total, dst_ref=six.at[place],
            send_sem=six_send.at[step - 1], recv_sem=six_recv.at[place],
            device_id=in_layer(z + step), device_id_type=MESH,
        )

    six_steps = [(3, 2), (2, 1)]
    for at, steps in enumerate(six_steps):
        @pl.when(place == at)
        def _(steps=steps):
            for step in steps:
                pl.semaphore_wait(ready.at[step], 1)
                six_copy(step).start()

    five_copy = pltpu.make_async_remote_copy(
        src_ref=total, dst_ref=five.at[0],
        send_sem=five_send, recv_sem=five_recv.at[0],
        device_id=in_layer(z + 1), device_id_type=MESH,
    )

    @pl.when(bits[5] == 0)
    def _():
        pl.semaphore_wait(ready.at[1], 1)
        five_copy.start()

    for n in range(4):
        sums[n] = groups[1][2 * n]
    sums[4], sums[5], sums[6] = groups[2][0], groups[2][2], groups[3][0]

    def low_source(level, xx):
        return {2: xx, 3: 4 + lax.div(xx, 2), 4: 6}[level]

    def low_copy(level, xx, yy):
        return pltpu.make_async_remote_copy(
            src_ref=sums.at[low_source(level, xx)], dst_ref=low.at[level - 1, mine],
            send_sem=lo_send.at[level - 2], recv_sem=lo_recv.at[level - 2],
            device_id=device(xx, yy, c), device_id_type=MESH,
        )

    for dx, dy in OFFSETS:
        xx, yy = xs[dx], ys[dy]
        for level, bit in ((2, lax.div(yy, 2)), (3, lax.rem(xx, 2)), (4, lax.div(xx, 2))):
            @pl.when(bit == 1)
            def _(level=level, xx=xx, yy=yy):
                low_copy(level, xx, yy).start()
    for level in (2, 3, 4):
        low[level - 1, mine] = sums[low_source(level, x)]

    def z_copy(layer):
        return pltpu.make_async_remote_copy(
            src_ref=total, dst_ref=zparts.at[z],
            send_sem=z_send.at[layer - 4], recv_sem=z_recv.at[z],
            device_id=in_layer(layer), device_id_type=MESH,
        )

    @pl.when(z < 4)
    def _():
        for layer in (7, 6, 5, 4):
            pl.semaphore_wait(ready.at[layer - z], 1)
            z_copy(layer).start()

    for b in range(SCALE_FIRST, 8):
        scale(b)

    def arrived(dst, sem):
        pltpu.make_async_remote_copy(
            src_ref=total, dst_ref=dst, send_sem=sem, recv_sem=sem, device_id=sibling, device_id_type=MESH
        ).wait_recv()

    def share(b, xx, yy):
        return pltpu.make_async_remote_copy(
            src_ref=zsum.at[b], dst_ref=high.at[b, mine],
            send_sem=hi_send.at[b], recv_sem=hi_recv.at[b],
            device_id=device(xx, yy, c), device_id_type=MESH,
        )

    def spread(b, sources, sems):
        @pl.when(bits[5 + b] == 1)
        def _():
            count = sources.shape[0]
            for n in range(count):
                arrived(sources.at[n], sems.at[n])
            values = [sources[n] for n in range(count)]
            while len(values) > 1:
                values = [values[i] + values[i + 1] for i in range(0, len(values), 2)]
            zsum[b] = values[0]
            for dx, dy in OFFSETS:
                share(b, xs[dx], ys[dy]).start()
            high[b, mine] = values[0]

    sources = ((five, five_recv), (six, six_recv), (zparts, z_recv))
    for b in HIGH_ORDER:
        spread(b, *sources[b])

    def low_forward(b):
        return pltpu.make_async_remote_copy(
            src_ref=low.at[b - 1, half], dst_ref=low.at[b - 1, half],
            send_sem=fw_send.at[2 + b], recv_sem=fw_recv.at[2 + b], device_id=sibling, device_id_type=MESH,
        )

    def high_forward(b):
        return pltpu.make_async_remote_copy(
            src_ref=high.at[b, half], dst_ref=high.at[b, half],
            send_sem=fw_send.at[b], recv_sem=fw_recv.at[b], device_id=sibling, device_id_type=MESH,
        )

    @pl.when(bits[1] == 1)
    def _():
        near_copy.wait_recv()
        low_forward(1).start()

    for b in (2, 3, 4):
        @pl.when(bits[b] == 1)
        def _(b=b):
            bytes_of(CHIPS - 1, lo_send.at[b - 2], lo_recv.at[b - 2]).wait_recv()
            low_forward(b).start()

    def high_wait(b):
        @pl.when(bits[5 + b] == 1)
        def _():
            bytes_of(CHIPS - 1, hi_send.at[b], hi_recv.at[b]).wait_recv()
            high_forward(b).start()

    def add_low(b):
        @pl.when(bits[b] == 1)
        def _():
            low_forward(b).wait_recv()
            add(b, lambda h: low[b - 1, head_chunks(h)])

    add_low(1)
    add_low(2)
    high_wait(HIGH_ORDER[0])
    add_low(3)
    high_wait(HIGH_ORDER[1])
    add_low(4)
    high_wait(HIGH_ORDER[2])

    for b in HIGH_ORDER:
        @pl.when(bits[5 + b] == 1)
        def _(b=b):
            high_forward(b).wait_recv()
            add(5 + b, lambda h: high[b, head_chunks(h)])

    other_copy.wait_send()
    bytes_of(CHIPS - 1, rs_send, rs_recv).wait_send()

    @pl.when(c == 0)
    def _():
        zero_copy.wait_send()

    for at, steps in enumerate(six_steps):
        @pl.when(place == at)
        def _(steps=steps):
            for step in steps:
                six_copy(step).wait_send()

    @pl.when(bits[5] == 0)
    def _():
        five_copy.wait_send()

    @pl.when(z < 4)
    def _():
        for layer in range(4, 8):
            z_copy(layer).wait_send()

    @pl.when(bits[1] == 0)
    def _():
        near_copy.wait_send()

    for b in (2, 3, 4):
        for bit in range(2):
            @pl.when(bits[b] == bit)
            def _(b=b, bit=bit):
                bytes_of(CHIPS // 2 - bit, lo_send.at[b - 2], lo_recv.at[b - 2]).wait_send()
    for b in range(1, 5):
        @pl.when(bits[b] == 1)
        def _(b=b):
            low_forward(b).wait_send()

    for b in range(3):
        @pl.when(bits[5 + b] == 1)
        def _(b=b):
            high_forward(b).wait_send()
            bytes_of(CHIPS - 1, hi_send.at[b], hi_recv.at[b]).wait_send()


def normalize(x_ref, o_hbm, out, sem):
    copies = []
    for n in range(SPANS):
        rows = slice(n * SPAN, (n + 1) * SPAN)
        for h in range(HEADS):
            cols = slice(h * HD, (h + 1) * HD)
            value = x_ref[rows, cols]
            square = jnp.mean(value * value, axis=-1, keepdims=True)
            out[rows, cols] = (value * lax.rsqrt(square + EPS)).astype(BF16)
        copies.append(pltpu.make_async_copy(out.at[rows], o_hbm.at[rows], sem.at[n]))
        copies[-1].start()
    for copy in copies:
        copy.wait()


def on_device(query_rows, key_rows, value_rows, level_ids, level_table):
    hbm = pl.BlockSpec(memory_space=pltpu.HBM)
    vmem = pl.BlockSpec(memory_space=pltpu.VMEM)
    dma = pltpu.SemaphoreType.DMA
    wide = (TOK, HEADS * HD)
    chunk = (CH, HD)
    unnormed = pl.pallas_call(
        kernel,
        out_shape=jax.ShapeDtypeStruct(wide, F32),
        in_specs=[hbm] * 5,
        out_specs=vmem,
        scratch_shapes=[
            pltpu.VMEM(wide, BF16),
            pltpu.VMEM(wide, BF16),
            pltpu.VMEM(wide, BF16),
            pltpu.VMEM((SPANS, SPAN), jnp.int32),
            pltpu.VMEM((CLASSES, HEADS, LEVELS), F32),
            pltpu.VMEM((CHUNKS, *chunk), F32),
            pltpu.VMEM((CHIPS, *chunk), F32),
            pltpu.VMEM((CHIPS, *chunk), F32),
            pltpu.VMEM((CHIPS, *chunk), F32),
            pltpu.VMEM((7, *chunk), F32),
            pltpu.VMEM(chunk, F32),
            pltpu.VMEM((1, *chunk), F32),
            pltpu.VMEM((2, *chunk), F32),
            pltpu.VMEM((4, *chunk), F32),
            pltpu.VMEM((3, *chunk), F32),
            pltpu.VMEM((CHIPS, *chunk), F32),
            pltpu.VMEM((4, CHUNKS, *chunk), F32),
            pltpu.VMEM((3, CHUNKS, *chunk), F32),
            pltpu.VMEM((TOK, LEVELS * HEADS), F32),
            pltpu.VMEM((8, *wide), BF16),
            dma((7,)), dma((2,)), dma, dma, dma((2,)), dma, dma, dma((3,)), dma((3,)), dma((3,)), dma((3,)),
            dma((7,)), dma((7,)),
            dma((4,)), dma((4,)), dma, dma((1,)), dma((3,)), dma((2,)), pltpu.SemaphoreType.REGULAR((LAYERS,)),
        ],
        compiler_params=pltpu.CompilerParams(
            collective_id=0, has_side_effects=True, vmem_limit_bytes=24 * 2**20
        ),
        name="fenwick",
    )(
        *[
            pltpu.with_memory_space_constraint(a, pltpu.HBM)
            for a in (
                query_rows, key_rows, value_rows,
                level_ids.reshape(SPANS, SPAN), jnp.transpose(level_table, (0, 2, 1)),
            )
        ]
    )
    return pl.pallas_call(
        normalize,
        out_shape=jax.ShapeDtypeStruct(wide, BF16),
        in_specs=[vmem],
        out_specs=hbm,
        scratch_shapes=[pltpu.VMEM(wide, BF16), dma((SPANS,))],
        compiler_params=pltpu.CompilerParams(vmem_limit_bytes=8 * 2**20),
        name="normalize",
    )(unnormed)


def solution(mesh):
    rows = P(("outer", "inner"), None)
    return jax.shard_map(
        on_device, mesh=mesh,
        in_specs=(rows, rows, rows, P(("outer", "inner")), P()),
        out_specs=rows, check_vma=False,
    )
```

```python
import jax
import jax.numpy as jnp
from jax import lax
from jax.experimental import pallas as pl
from jax.experimental.pallas import tpu as pltpu
from jax.sharding import PartitionSpec as P

HEADS = 4
HD = 128
SPAN = 128
LEVELS = 16
CLASSES = 16
TOK = 512
SPANS = TOK // SPAN
CHIPS = 16
LAYERS = 8
CHUNKS = 2 * CHIPS
CH = HEADS * HD // CHUNKS
PER_HEAD = CHUNKS // HEADS
HALF = HEADS * HD // 2
EPS = 1e-06
MESH = pl.DeviceIdType.MESH
F32 = jnp.float32
BF16 = jnp.bfloat16

OFFSETS = sorted(
    ((dx, dy) for dx in range(4) for dy in range(4) if dx or dy),
    key=lambda o: -(min(o[0], 4 - o[0]) + min(o[1], 4 - o[1])),
)
STEPS = sorted(range(1, LAYERS), key=lambda s: -min(s, LAYERS - s))
SCALE_FIRST = 6
HIGH_ORDER = (0, 2, 1)


def kernel(
    q_hbm, k_hbm, v_hbm, ids_hbm, table_hbm, acc,
    q, k, v, ids, table, state, other, chip_state, parts, sums, total, five, six, zparts, zsum, zero, low, high,
    lam, scaled,
    in_sem, other_sem, rs_send, rs_recv, zero_sem, y_send, y_recv, lo_send, lo_recv, hi_send, hi_recv, fw_send, fw_recv,
    z_send, z_recv, five_send, five_recv, six_send, six_recv, ready,
):
    outer = lax.axis_index("outer")
    inner = lax.axis_index("inner")
    z, x = lax.div(outer, 4), lax.rem(outer, 4)
    y, c = lax.div(inner, 2), lax.rem(inner, 2)
    p = x * 4 + y
    place = lax.rem(z, 4)
    mine = c * CHIPS + p
    xs = [lax.rem(x + dx, 4) for dx in range(4)]
    ys = [lax.rem(y + dy, 4) for dy in range(4)]

    def device(xx, yy, cc, layer=None):
        return {"outer": (z if layer is None else layer) * 4 + xx, "inner": yy * 2 + cc}

    sibling = device(x, y, 1 - c)

    def in_layer(layer):
        return {"outer": layer * 4 + x, "inner": inner}

    def columns(cc):
        return pl.ds(pl.multiple_of(cc * HALF, HALF), HALF)

    def load(src, dst, n):
        return pltpu.make_async_copy(src, dst, in_sem.at[n])

    key_loads = [
        [
            load(src.at[:, columns(cc)], dst.at[:, columns(cc)], 2 * n + i)
            for i, (src, dst) in enumerate(((k_hbm, k), (v_hbm, v)))
        ]
        for n, cc in enumerate((1 - c, c))
    ]
    late_loads = [load(ids_hbm, ids, 4), load(table_hbm, table, 5), load(q_hbm, q, 6)]
    for copy in key_loads[0] + key_loads[1] + late_loads:
        copy.start()

    barrier = pltpu.get_barrier_semaphore()

    def greet(dev):
        pl.semaphore_signal(barrier, inc=1, device_id=dev, device_id_type=MESH)

    for dx, dy in OFFSETS:
        greet(device(xs[dx], ys[dy], c))
    greet(sibling)
    for step in STEPS:
        @pl.when(z + step < LAYERS)
        def _(step=step):
            greet(in_layer(z + step))

    def head(h):
        return slice(h * HD, (h + 1) * HD)

    def head_chunks(h):
        return slice(h * PER_HEAD, (h + 1) * PER_HEAD)

    def contract_tokens(a, b):
        return lax.dot_general(a, b, (((0,), (0,)), ((), ())), preferred_element_type=F32)

    def half_state(n, cc, sends=()):
        for copy in key_loads[n]:
            copy.wait()
        for i in range(HEADS // 2):
            cols = pl.ds(pl.multiple_of(cc * HALF + i * HD, HD), HD)
            value = contract_tokens(k[:, cols], v[:, cols])
            state[pl.ds(cc * CHIPS + i * PER_HEAD, PER_HEAD)] = value.reshape(PER_HEAD, CH, HD)
            if sends:
                if i == 0:
                    pl.semaphore_wait(barrier, CHIPS - 1 + 1 + z)
                sends[i].start()

    half = pl.ds(c * CHIPS, CHIPS)
    other_copies = [
        pltpu.make_async_remote_copy(
            src_ref=state.at[pl.ds((1 - c) * CHIPS + i * PER_HEAD, PER_HEAD)],
            dst_ref=other.at[pl.ds(i * PER_HEAD, PER_HEAD)],
            send_sem=other_sem.at[2 * i], recv_sem=other_sem.at[2 * i + 1],
            device_id=sibling, device_id_type=MESH,
        )
        for i in range(HEADS // 2)
    ]
    half_state(0, 1 - c, other_copies)
    half_state(1, c)

    for step in STEPS:
        @pl.when(step <= z)
        def _(step=step):
            pl.semaphore_signal(ready.at[step], inc=1, device_id=in_layer(z - step), device_id_type=MESH)

    for copy in other_copies:
        copy.wait_recv()
    chip_state[...] = state[half] + other[...]

    def to_owner(xx, yy):
        return pltpu.make_async_remote_copy(
            src_ref=chip_state.at[xx * 4 + yy], dst_ref=parts.at[p],
            send_sem=rs_send, recv_sem=rs_recv,
            device_id=device(xx, yy, c), device_id_type=MESH,
        )

    for dx, dy in OFFSETS:
        to_owner(xs[dx], ys[dy]).start()
    parts[p] = chip_state[p]

    bits = (
        [c]
        + [lax.rem(lax.div(p, 2**b), 2) for b in range(4)]
        + [lax.rem(lax.div(z, 2**b), 2) for b in range(3)]
    )
    near_copy = pltpu.make_async_remote_copy(
        src_ref=chip_state, dst_ref=low.at[0, half], send_sem=y_send, recv_sem=y_recv,
        device_id=device(x, lax.rem(y + 1, 4), c), device_id_type=MESH,
    )

    @pl.when(bits[1] == 0)
    def _():
        near_copy.start()

    zero_copy = pltpu.make_async_remote_copy(
        src_ref=state.at[pl.ds(0, CHIPS)], dst_ref=zero, send_sem=zero_sem.at[0], recv_sem=zero_sem.at[1],
        device_id=sibling, device_id_type=MESH,
    )

    @pl.when(c == 0)
    def _():
        zero_copy.start()

    for copy in late_loads:
        copy.wait()
    classes = lax.broadcasted_iota(jnp.int32, (CLASSES, SPAN), 0)
    causal = lax.broadcasted_iota(jnp.int32, (SPAN, SPAN), 0) >= lax.broadcasted_iota(
        jnp.int32, (SPAN, SPAN), 1
    )
    span_rows = [slice(n * SPAN, (n + 1) * SPAN) for n in range(SPANS)]
    for n in range(SPANS):
        hot = (ids[n : n + 1, :] == classes).astype(F32)
        for h in range(HEADS):
            lam[span_rows[n], h * LEVELS : (h + 1) * LEVELS] = lax.dot_general(
                hot, table[:, h, :], (((0,), (0,)), ((), ())),
                precision=lax.Precision.HIGHEST, preferred_element_type=F32,
            )

    def weight(rows, level, h):
        n = h * LEVELS + level
        return lam[rows, n : n + 1]

    for h in range(HEADS):
        spans = [contract_tokens(k[span_rows[n], head(h)], v[span_rows[n], head(h)]) for n in range(3)]
        first = [None, spans[0].astype(BF16), None, spans[2].astype(BF16)]
        second = (spans[0] + spans[1]).astype(BF16)
        for n in range(SPANS):
            rows = span_rows[n]
            q_now = q[rows, head(h)]
            scores = lax.dot_general(
                q_now, k[rows, head(h)], (((1,), (1,)), ((), ())), preferred_element_type=F32
            )
            weighted = jnp.where(causal, scores * weight(rows, 0, h), 0.0).astype(BF16)
            out = jnp.dot(weighted, v[rows, head(h)], preferred_element_type=F32)
            if n % 2 == 1:
                out += weight(rows, 1, h) * jnp.dot(q_now, first[n], preferred_element_type=F32)
            if n >= 2:
                out += weight(rows, 2, h) * jnp.dot(q_now, second, preferred_element_type=F32)
            acc[rows, head(h)] = out

    def scale(b):
        @pl.when(bits[b] == 1)
        def _():
            for h in range(HEADS):
                scaled[b, :, head(h)] = (q[:, head(h)].astype(F32) * weight(slice(0, TOK), 3 + b, h)).astype(BF16)

    for b in range(SCALE_FIRST):
        scale(b)

    def bytes_of(n, send_sem, recv_sem):
        return pltpu.make_async_remote_copy(
            src_ref=state.at[pl.ds(0, n)], dst_ref=state.at[pl.ds(0, n)],
            send_sem=send_sem, recv_sem=recv_sem, device_id=sibling, device_id_type=MESH,
        )

    bytes_of(CHIPS - 1, rs_send, rs_recv).wait_recv()
    groups = [[parts[n] for n in range(CHIPS)]]
    for b in range(4):
        below = groups[-1]
        groups.append([below[2 * n] + below[2 * n + 1] for n in range(len(below) // 2)])
    total[...] = groups[4][0]

    def six_copy(step):
        return pltpu.make_async_remote_copy(
            src_ref=total, dst_ref=six.at[place],
            send_sem=six_send.at[step - 1], recv_sem=six_recv.at[place],
            device_id=in_layer(z + step), device_id_type=MESH,
        )

    six_steps = [(3, 2), (2, 1)]
    for at, steps in enumerate(six_steps):
        @pl.when(place == at)
        def _(steps=steps):
            for step in steps:
                pl.semaphore_wait(ready.at[step], 1)
                six_copy(step).start()

    five_copy = pltpu.make_async_remote_copy(
        src_ref=total, dst_ref=five.at[0],
        send_sem=five_send, recv_sem=five_recv.at[0],
        device_id=in_layer(z + 1), device_id_type=MESH,
    )

    @pl.when(bits[5] == 0)
    def _():
        pl.semaphore_wait(ready.at[1], 1)
        five_copy.start()

    for n in range(4):
        sums[n] = groups[1][2 * n]
    sums[4], sums[5], sums[6] = groups[2][0], groups[2][2], groups[3][0]

    def low_source(level, xx):
        return {2: xx, 3: 4 + lax.div(xx, 2), 4: 6}[level]

    def low_copy(level, xx, yy):
        return pltpu.make_async_remote_copy(
            src_ref=sums.at[low_source(level, xx)], dst_ref=low.at[level - 1, mine],
            send_sem=lo_send.at[level - 2], recv_sem=lo_recv.at[level - 2],
            device_id=device(xx, yy, c), device_id_type=MESH,
        )

    for dx, dy in OFFSETS:
        xx, yy = xs[dx], ys[dy]
        for level, bit in ((2, lax.div(yy, 2)), (3, lax.rem(xx, 2)), (4, lax.div(xx, 2))):
            @pl.when(bit == 1)
            def _(level=level, xx=xx, yy=yy):
                low_copy(level, xx, yy).start()
    for level in (2, 3, 4):
        low[level - 1, mine] = sums[low_source(level, x)]

    def z_copy(layer):
        return pltpu.make_async_remote_copy(
            src_ref=total, dst_ref=zparts.at[z],
            send_sem=z_send.at[layer - 4], recv_sem=z_recv.at[z],
            device_id=in_layer(layer), device_id_type=MESH,
        )

    @pl.when(z < 4)
    def _():
        for layer in (7, 6, 5, 4):
            pl.semaphore_wait(ready.at[layer - z], 1)
            z_copy(layer).start()

    for b in range(SCALE_FIRST, 8):
        scale(b)

    def arrived(dst, sem):
        pltpu.make_async_remote_copy(
            src_ref=total, dst_ref=dst, send_sem=sem, recv_sem=sem, device_id=sibling, device_id_type=MESH
        ).wait_recv()

    def share(b, xx, yy):
        return pltpu.make_async_remote_copy(
            src_ref=zsum.at[b], dst_ref=high.at[b, mine],
            send_sem=hi_send.at[b], recv_sem=hi_recv.at[b],
            device_id=device(xx, yy, c), device_id_type=MESH,
        )

    def spread(b, sources, sems):
        @pl.when(bits[5 + b] == 1)
        def _():
            count = sources.shape[0]
            for n in range(count):
                arrived(sources.at[n], sems.at[n])
            values = [sources[n] for n in range(count)]
            while len(values) > 1:
                values = [values[i] + values[i + 1] for i in range(0, len(values), 2)]
            zsum[b] = values[0]
            for dx, dy in OFFSETS:
                share(b, xs[dx], ys[dy]).start()
            high[b, mine] = values[0]

    sources = ((five, five_recv), (six, six_recv), (zparts, z_recv))
    for b in HIGH_ORDER:
        spread(b, *sources[b])

    def low_forward(b):
        return pltpu.make_async_remote_copy(
            src_ref=low.at[b - 1, half], dst_ref=low.at[b - 1, half],
            send_sem=fw_send.at[2 + b], recv_sem=fw_recv.at[2 + b], device_id=sibling, device_id_type=MESH,
        )

    def high_forward(b):
        return pltpu.make_async_remote_copy(
            src_ref=high.at[b, half], dst_ref=high.at[b, half],
            send_sem=fw_send.at[b], recv_sem=fw_recv.at[b], device_id=sibling, device_id_type=MESH,
        )

    def add(b, matrix):
        for h in range(HEADS):
            acc[:, head(h)] += jnp.dot(
                scaled[b, :, head(h)], matrix(h).reshape(HD, HD).astype(BF16), preferred_element_type=F32
            )

    @pl.when(bits[1] == 1)
    def _():
        near_copy.wait_recv()
        low_forward(1).start()

    for b in (2, 3, 4):
        @pl.when(bits[b] == 1)
        def _(b=b):
            bytes_of(CHIPS - 1, lo_send.at[b - 2], lo_recv.at[b - 2]).wait_recv()
            low_forward(b).start()

    def high_wait(b):
        @pl.when(bits[5 + b] == 1)
        def _():
            bytes_of(CHIPS - 1, hi_send.at[b], hi_recv.at[b]).wait_recv()
            high_forward(b).start()

    @pl.when(c == 1)
    def _():
        zero_copy.wait_recv()
        add(0, lambda h: (zero if h < 2 else other)[head_chunks(h % 2)])

    def add_low(b):
        @pl.when(bits[b] == 1)
        def _():
            low_forward(b).wait_recv()
            add(b, lambda h: low[b - 1, head_chunks(h)])

    add_low(1)
    add_low(2)
    high_wait(HIGH_ORDER[0])
    add_low(3)
    high_wait(HIGH_ORDER[1])
    add_low(4)
    high_wait(HIGH_ORDER[2])

    for b in HIGH_ORDER:
        @pl.when(bits[5 + b] == 1)
        def _(b=b):
            high_forward(b).wait_recv()
            add(5 + b, lambda h: high[b, head_chunks(h)])

    for copy in other_copies:
        copy.wait_send()
    bytes_of(CHIPS - 1, rs_send, rs_recv).wait_send()

    @pl.when(c == 0)
    def _():
        zero_copy.wait_send()

    for at, steps in enumerate(six_steps):
        @pl.when(place == at)
        def _(steps=steps):
            for step in steps:
                six_copy(step).wait_send()

    @pl.when(bits[5] == 0)
    def _():
        five_copy.wait_send()

    @pl.when(z < 4)
    def _():
        for layer in range(4, 8):
            z_copy(layer).wait_send()

    @pl.when(bits[1] == 0)
    def _():
        near_copy.wait_send()

    for b in (2, 3, 4):
        for bit in range(2):
            @pl.when(bits[b] == bit)
            def _(b=b, bit=bit):
                bytes_of(CHIPS // 2 - bit, lo_send.at[b - 2], lo_recv.at[b - 2]).wait_send()
    for b in range(1, 5):
        @pl.when(bits[b] == 1)
        def _(b=b):
            low_forward(b).wait_send()

    for b in range(3):
        @pl.when(bits[5 + b] == 1)
        def _(b=b):
            high_forward(b).wait_send()
            bytes_of(CHIPS - 1, hi_send.at[b], hi_recv.at[b]).wait_send()


def normalize(x_ref, o_hbm, out, sem):
    copies = []
    for n in range(SPANS):
        rows = slice(n * SPAN, (n + 1) * SPAN)
        for h in range(HEADS):
            cols = slice(h * HD, (h + 1) * HD)
            value = x_ref[rows, cols]
            square = jnp.mean(value * value, axis=-1, keepdims=True)
            out[rows, cols] = (value * lax.rsqrt(square + EPS)).astype(BF16)
        copies.append(pltpu.make_async_copy(out.at[rows], o_hbm.at[rows], sem.at[n]))
        copies[-1].start()
    for copy in copies:
        copy.wait()


def on_device(query_rows, key_rows, value_rows, level_ids, level_table):
    hbm = pl.BlockSpec(memory_space=pltpu.HBM)
    vmem = pl.BlockSpec(memory_space=pltpu.VMEM)
    dma = pltpu.SemaphoreType.DMA
    wide = (TOK, HEADS * HD)
    chunk = (CH, HD)
    unnormed = pl.pallas_call(
        kernel,
        out_shape=jax.ShapeDtypeStruct(wide, F32),
        in_specs=[hbm] * 5,
        out_specs=vmem,
        scratch_shapes=[
            pltpu.VMEM(wide, BF16),
            pltpu.VMEM(wide, BF16),
            pltpu.VMEM(wide, BF16),
            pltpu.VMEM((SPANS, SPAN), jnp.int32),
            pltpu.VMEM((CLASSES, HEADS, LEVELS), F32),
            pltpu.VMEM((CHUNKS, *chunk), F32),
            pltpu.VMEM((CHIPS, *chunk), F32),
            pltpu.VMEM((CHIPS, *chunk), F32),
            pltpu.VMEM((CHIPS, *chunk), F32),
            pltpu.VMEM((7, *chunk), F32),
            pltpu.VMEM(chunk, F32),
            pltpu.VMEM((1, *chunk), F32),
            pltpu.VMEM((2, *chunk), F32),
            pltpu.VMEM((4, *chunk), F32),
            pltpu.VMEM((3, *chunk), F32),
            pltpu.VMEM((CHIPS, *chunk), F32),
            pltpu.VMEM((4, CHUNKS, *chunk), F32),
            pltpu.VMEM((3, CHUNKS, *chunk), F32),
            pltpu.VMEM((TOK, LEVELS * HEADS), F32),
            pltpu.VMEM((8, *wide), BF16),
            dma((7,)), dma((4,)), dma, dma, dma((2,)), dma, dma, dma((3,)), dma((3,)), dma((3,)), dma((3,)),
            dma((7,)), dma((7,)),
            dma((4,)), dma((4,)), dma, dma((1,)), dma((3,)), dma((2,)), pltpu.SemaphoreType.REGULAR((LAYERS,)),
        ],
        compiler_params=pltpu.CompilerParams(
            collective_id=0, has_side_effects=True, vmem_limit_bytes=24 * 2**20
        ),
        name="fenwick",
    )(
        *[
            pltpu.with_memory_space_constraint(a, pltpu.HBM)
            for a in (
                query_rows, key_rows, value_rows,
                level_ids.reshape(SPANS, SPAN), jnp.transpose(level_table, (0, 2, 1)),
            )
        ]
    )
    return pl.pallas_call(
        normalize,
        out_shape=jax.ShapeDtypeStruct(wide, BF16),
        in_specs=[vmem],
        out_specs=hbm,
        scratch_shapes=[pltpu.VMEM(wide, BF16), dma((SPANS,))],
        compiler_params=pltpu.CompilerParams(vmem_limit_bytes=8 * 2**20),
        name="normalize",
    )(unnormed)


def solution(mesh):
    rows = P(("outer", "inner"), None)
    return jax.shard_map(
        on_device, mesh=mesh,
        in_specs=(rows, rows, rows, P(("outer", "inner")), P()),
        out_specs=rows, check_vma=False,
    )
```
